32 devices in a mesh: ctx: 8 (over z, y), shard: 4 (over x, core).
Axes of the slice: x: 2, y: 2, z: 4, core: 2. Of those that a mesh axis runs over, the one named last changes fastest.
Arguments:
- tokens: bfloat16 [4, 1024, 1024], P('shard', 'ctx'), may hold values from -6 to 6
- cotangent: float32 [4, 1024, 1024], P('shard', 'ctx'), may hold values from -6 to 6
- lengths: int32 [4], P('shard'), may hold values from 512 to 1024, as said below
- matrices: bfloat16 [1024, 12288], P(('ctx', 'shard'))
- vectors: bfloat16 [12, 1024], P(None, ('ctx', 'shard'))
- first_moment: float32 [1024, 12288], P(('ctx', 'shard')), may hold values from -6 to 6
- second_moment: float32 [1024, 12288], P(('ctx', 'shard')), may hold values from 1 to 100
- vec_first: float32 [12, 1024], P(None, ('ctx', 'shard')), may hold values from -6 to 6
- vec_second: float32 [12, 1024], P(None, ('ctx', 'shard')), may hold values from 1 to 100
Outputs:
- outputs: float32 [4, 1024, 1024], P('shard', 'ctx')
- grad_input: float32 [4, 1024, 1024], P('shard', 'ctx')
- grad_matrices: float32 [1024, 12288], P(('ctx', 'shard'))
- grad_vectors: float32 [12, 1024], P(None, ('ctx', 'shard'))
- new_matrices: float32 [1024, 12288], P(('ctx', 'shard'))
- new_vectors: float32 [12, 1024], P(None, ('ctx', 'shard'))
- new_first: float32 [1024, 12288], P(('ctx', 'shard'))
- new_second: float32 [1024, 12288], P(('ctx', 'shard'))
- new_vec_first: float32 [12, 1024], P(None, ('ctx', 'shard'))
- new_vec_second: float32 [12, 1024], P(None, ('ctx', 'shard'))
The draws below stay inside these ranges and needn't reach their ends.
Inputs may be any that keep to these rules, and one draw needn't show every extreme that they name: lengths counts the real tokens of each sequence; at least one sequence has no padding.
All inputs are finite; a program needn't handle non-finite values.
Results may differ from the reference program's by a relative error of at most 0.014.
Values may be sent and summed in bfloat16 or wider, within the bound.
No kernel may reach another device: no remote copies, remote signals or barrier semaphores. Data moves between devices by JAX's collectives and lax.ppermute only.
A program may use at most 320 MiB of HBM per device.

```python
import math
import jax
import jax.numpy as jnp
from jax import lax

D = 1024
HEADS = 16
HDIM = 64
FF = 4096
STEP = 5
LENGTH = 1024
SEQS = 4
NCOL = 12288
VROWS = 12


def draw_lengths(key, part):
    base_lengths = jax.random.randint(jax.random.fold_in(key, 11), (SEQS,), LENGTH // 2, LENGTH + 1)
    chosen = jax.random.randint(jax.random.fold_in(key, 12), (), 0, SEQS)
    return jnp.where(jnp.arange(SEQS) == chosen, LENGTH, base_lengths).astype(jnp.int32)


def draw_matrices(key, part):
    columns = jnp.arange(4 * D + 2 * FF)
    column_scale = jnp.where(columns < 3 * D, D ** (-0.5), jnp.where(columns < 4 * D, D ** (-0.5) * LENGTH ** 0.5 / 2.0, jnp.where(columns < 4 * D + FF, D ** (-0.5), FF ** (-0.5))))
    raw_values = jax.random.normal(key, (D, 4 * D + 2 * FF), jnp.float32)
    return (raw_values * column_scale[None, :]).astype(jnp.bfloat16)


def draw_vectors(key, part):
    row_ids = jnp.arange(8 + FF // D)[:, None]
    noise = jnp.clip(jax.random.normal(key, (8 + FF // D, D), jnp.float32), -4.0, 4.0)
    gain_rows = (row_ids == 3) | (row_ids == 6)
    row_scale = jnp.where(row_ids == 1, 0.015, 0.5)
    return jnp.where(gain_rows, 1.0 + 0.2 * noise, row_scale * noise).astype(jnp.bfloat16)


def level_of(key, shape, cuts, smallest, largest):
    factor_of = 1.0
    for dim, parts in cuts:
        draws = jax.random.uniform(jax.random.fold_in(jax.random.fold_in(key, 6), dim), (parts,), jnp.float32, smallest / len(cuts), largest / len(cuts))
        factor_of = factor_of * jnp.repeat(jnp.exp(draws), shape[dim] // parts).reshape((-1,) + (1,) * (len(shape) - 1 - dim))
    return factor_of


def bell_draw(key, extent, spread, bound, pieces=(), held_as=jnp.bfloat16):
    result = spread * jax.random.normal(key, extent, jnp.float32)
    if pieces:
        result = result * level_of(key, extent, pieces, -0.22, 0.18)
    return jnp.clip(result, -bound, bound).astype(held_as)


def setup_inputs(seed: int = 0) -> dict:
    splits = jax.random.split(jax.random.key(seed), 10)
    return {
        "tokens": bell_draw(splits[0], (SEQS, LENGTH, D), 1.0, 6.0, ((0, 4), (1, 8))),
        "cotangent": bell_draw(splits[1], (SEQS, LENGTH, D), 1.0, 6.0, ((0, 4), (1, 8)), jnp.float32),
        "lengths": draw_lengths(jax.random.fold_in(splits[9], 71), 0),
        "matrices": draw_matrices(jax.random.fold_in(splits[9], 71), 0),
        "vectors": draw_vectors(jax.random.fold_in(splits[9], 71), 0),
        "first_moment": bell_draw(splits[5], (D, NCOL), 1.0, 6.0, ((0, 32),), jnp.float32),
        "second_moment": jnp.clip(jnp.exp(math.log(100.0) - 4.6051702 * jax.random.uniform(splits[6], (D, NCOL), jnp.float32) ** level_of(splits[6], (D, NCOL), ((0, 32),), -0.2, 0.2)), 1.0, 100.0),
        "vec_first": bell_draw(splits[7], (VROWS, D), 1.0, 6.0, ((1, 32),), jnp.float32),
        "vec_second": jnp.clip(jnp.exp(math.log(100.0) - 4.6051702 * jax.random.uniform(splits[8], (VROWS, D), jnp.float32) ** level_of(splits[8], (VROWS, D), ((1, 32),), -0.2, 0.2)), 1.0, 100.0),
    }


beta_first = 0.9
beta_second = 0.999
learn_rate = 0.02
decay_rate = 0.01
adam_eps = 1e-08
norm_eps = 1e-06

def norm_forward(resid, gain_row, shift_row):
    centered = resid - lax.optimization_barrier(jnp.mean(resid, axis=-1, keepdims=True))
    inverse = lax.rsqrt(lax.optimization_barrier(jnp.mean(centered * centered, axis=-1, keepdims=True)) + norm_eps)
    normed = centered * inverse
    return (normed * gain_row + shift_row, normed, inverse)

def norm_backward(upstream, gain_row, normed, inverse):
    scaled = upstream * gain_row
    return inverse * (scaled - lax.optimization_barrier(jnp.mean(scaled, axis=-1, keepdims=True)) - normed * lax.optimization_barrier(jnp.mean(scaled * normed, axis=-1, keepdims=True)))

def gelu_parts(preact):
    cumulative = 0.5 * (1.0 + lax.erf(preact * 0.7071067811865476))
    density = jnp.exp(-0.5 * preact * preact) * 0.3989422804014327
    return (preact * cumulative, cumulative + preact * density)

def contract_rows(left, right):
    return lax.dot_general(left, right, (((0,), (0,)), ((), ())), preferred_element_type=jnp.float32)

def contract_cols(left, right):
    return lax.dot_general(left, right, (((1,), (1,)), ((), ())), preferred_element_type=jnp.float32)

def adam_update(weights, grads, first, second, decay):
    new_first = beta_first * first + (1.0 - beta_first) * grads
    new_second = beta_second * second + (1.0 - beta_second) * grads * grads
    corr_first = 1.0 - beta_first ** STEP
    corr_second = 1.0 - beta_second ** STEP
    update = new_first / corr_first / (jnp.sqrt(new_second / corr_second) + adam_eps)
    new_weights = weights.astype(jnp.float32) * (1.0 - learn_rate * decay) - learn_rate * update
    return (new_weights, new_first, new_second)

def head_slice(array, head):
    return lax.dynamic_slice_in_dim(array, (head * HDIM).astype(jnp.int32), HDIM, 1)

def attention_forward(queries, keys, values, valid_keys):

    def one_head(head):
        query_h = head_slice(queries, head)
        key_h = head_slice(keys, head)
        value_h = head_slice(values, head)
        scores = jnp.dot(query_h, key_h.T, preferred_element_type=jnp.float32)
        logsum = jnp.log(lax.optimization_barrier(jnp.sum(jnp.where(valid_keys, jnp.exp(scores), 0.0), axis=1)))
        attn_probs = jnp.where(valid_keys, jnp.exp(scores - logsum[:, None]), 0.0).astype(jnp.bfloat16)
        head_out = jnp.dot(attn_probs, value_h, preferred_element_type=jnp.float32).astype(jnp.bfloat16)
        return (head_out, logsum)
    head_outs, logsums = lax.map(one_head, jnp.arange(HEADS, dtype=jnp.int32))
    seq_rows = queries.shape[0]
    return (head_outs.transpose(1, 0, 2).reshape(seq_rows, HEADS * HDIM), logsums)

def attention_backward(queries, keys, values, mixed, grad_mixed, logsums, valid_keys):
    head_scale = HDIM ** (-0.5)

    def one_head(items):
        head, logsum = items
        query_h = head_slice(queries, head)
        key_h = head_slice(keys, head)
        value_h = head_slice(values, head)
        mixed_h = head_slice(mixed, head)
        grad_h = head_slice(grad_mixed, head)
        scores = jnp.dot(query_h, key_h.T, preferred_element_type=jnp.float32)
        probs_full = jnp.where(valid_keys, jnp.exp(scores - logsum[:, None]), 0.0)
        probs_low = probs_full.astype(jnp.bfloat16)
        grad_probs = jnp.dot(grad_h, value_h.T, preferred_element_type=jnp.float32)
        row_delta = lax.optimization_barrier(jnp.sum(grad_h.astype(jnp.float32) * mixed_h.astype(jnp.float32), axis=1))
        grad_scores = (probs_full * (grad_probs - row_delta[:, None])).astype(jnp.bfloat16)
        grad_query = jnp.dot(grad_scores, key_h, preferred_element_type=jnp.float32) * head_scale
        grad_key = contract_rows(grad_scores, query_h)
        grad_value = contract_rows(probs_low, grad_h)
        return (grad_query, grad_key, grad_value)
    stacked = lax.map(one_head, (jnp.arange(HEADS, dtype=jnp.int32), logsums))
    seq_rows = queries.shape[0]
    return tuple((piece.transpose(1, 0, 2).reshape(seq_rows, HEADS * HDIM) for piece in stacked))

def layer_pass(inputs, upstream, length, matrices, vector_rows):
    width = inputs.shape[1]
    hidden_width = (matrices.shape[1] - 4 * width) // 2
    weight_qkv = matrices[:, :3 * width]
    weight_out = matrices[:, 3 * width:4 * width]
    weight_up = matrices[:, 4 * width:4 * width + hidden_width]
    weight_down = matrices[:, 4 * width + hidden_width:]
    bias_up = vector_rows[8:].reshape(-1)
    head_scale = HDIM ** (-0.5)
    projected = jnp.dot(inputs, weight_qkv, preferred_element_type=jnp.float32)
    queries = ((projected[:, :width] + vector_rows[0]) * head_scale).astype(jnp.bfloat16)
    keys = projected[:, width:2 * width].astype(jnp.bfloat16)
    values = (projected[:, 2 * width:] + vector_rows[1]).astype(jnp.bfloat16)
    valid_keys = jnp.arange(inputs.shape[0], dtype=jnp.int32) < length
    mixed, logsums = attention_forward(queries, keys, values, valid_keys)
    resid_one = inputs.astype(jnp.float32) + jnp.dot(mixed, weight_out, preferred_element_type=jnp.float32) + vector_rows[2]
    hidden, normed_one, inverse_one = norm_forward(resid_one, vector_rows[3], vector_rows[4])
    hidden_low = hidden.astype(jnp.bfloat16)
    preact = jnp.dot(hidden_low, weight_up, preferred_element_type=jnp.float32) + bias_up
    activ_full, gelu_slope = gelu_parts(preact)
    activated = activ_full.astype(jnp.bfloat16)
    resid_two = hidden + contract_cols(activated, weight_down) + vector_rows[5]
    outputs, normed_two, inverse_two = norm_forward(resid_two, vector_rows[6], vector_rows[7])
    grad_resid_two = norm_backward(upstream, vector_rows[6], normed_two, inverse_two)
    grad_two_low = grad_resid_two.astype(jnp.bfloat16)
    grad_preact = jnp.dot(grad_two_low, weight_down, preferred_element_type=jnp.float32) * gelu_slope
    grad_preact_low = grad_preact.astype(jnp.bfloat16)
    grad_hidden = grad_resid_two + contract_cols(grad_preact_low, weight_up)
    grad_resid_one = norm_backward(grad_hidden, vector_rows[3], normed_one, inverse_one)
    grad_one_low = grad_resid_one.astype(jnp.bfloat16)
    grad_mixed = contract_cols(grad_one_low, weight_out).astype(jnp.bfloat16)
    grad_query, grad_key, grad_value = attention_backward(queries, keys, values, mixed, grad_mixed, logsums, valid_keys)
    grad_proj = jnp.concatenate([grad_query, grad_key, grad_value], axis=1).astype(jnp.bfloat16)
    grad_input = grad_resid_one + contract_cols(grad_proj, weight_qkv)
    grad_term = jnp.concatenate([contract_rows(inputs, grad_proj), contract_rows(mixed, grad_one_low), contract_rows(hidden_low, grad_preact_low), contract_rows(grad_two_low, activated)], axis=1)
    small_rows = jnp.stack([lax.optimization_barrier(jnp.sum(grad_query, axis=0)), lax.optimization_barrier(jnp.sum(grad_value, axis=0)), lax.optimization_barrier(jnp.sum(grad_resid_one, axis=0)), lax.optimization_barrier(jnp.sum(grad_hidden * normed_one, axis=0)), lax.optimization_barrier(jnp.sum(grad_hidden, axis=0)), lax.optimization_barrier(jnp.sum(grad_resid_two, axis=0)), lax.optimization_barrier(jnp.sum(upstream * normed_two, axis=0)), lax.optimization_barrier(jnp.sum(upstream, axis=0))])
    vec_term = jnp.concatenate([small_rows, lax.optimization_barrier(jnp.sum(grad_preact, axis=0)).reshape(-1, width)], axis=0)
    return (outputs, grad_input, grad_term, vec_term)

def reference(tokens, cotangent, lengths, matrices, vectors, first_moment, second_moment, vec_first, vec_second):
    vector_rows = vectors.astype(jnp.float32)

    def one_sequence(carry, items):
        inputs, upstream, length = items
        outputs, grad_input, grad_term, vec_term = layer_pass(inputs, upstream, length, matrices, vector_rows)
        return ((carry[0] + grad_term, carry[1] + vec_term), (outputs, grad_input))
    start_sums = (jnp.zeros(matrices.shape, jnp.float32), jnp.zeros(vectors.shape, jnp.float32))
    sums, results = lax.scan(one_sequence, start_sums, (tokens, cotangent, lengths))
    grad_matrices, grad_vectors = sums
    outputs, grad_input = results
    new_matrices, new_first, new_second = adam_update(matrices, grad_matrices, first_moment, second_moment, decay_rate)
    new_vectors, new_vec_first, new_vec_second = adam_update(vectors, grad_vectors, vec_first, vec_second, 0.0)
    return (outputs, grad_input, grad_matrices, grad_vectors, new_matrices, new_vectors, new_first, new_second, new_vec_first, new_vec_second)
```

```python
import functools

import jax
import jax.numpy as jnp
from jax import lax
from jax.experimental import pallas as pl
from jax.experimental.pallas import tpu as pltpu
from jax.sharding import Mesh, PartitionSpec as P


HDIM = 64
STEP = 5


beta_first = 0.9
beta_second = 0.999
learn_rate = 0.02
decay_rate = 0.01
adam_eps = 1e-08
norm_eps = 1e-06


def norm_forward(resid, gain_row, shift_row):
    centered = resid - jnp.mean(resid, axis=-1, keepdims=True)
    inverse = lax.rsqrt(jnp.mean(centered * centered, axis=-1, keepdims=True) + norm_eps)
    normed = centered * inverse
    return (normed * gain_row + shift_row, normed, inverse)


def norm_backward(upstream, gain_row, normed, inverse):
    scaled = upstream * gain_row
    return inverse * (
        scaled
        - jnp.mean(scaled, axis=-1, keepdims=True)
        - normed * jnp.mean(scaled * normed, axis=-1, keepdims=True)
    )


def gelu_parts(preact):
    cumulative = 0.5 * (1.0 + lax.erf(preact * 0.7071067811865476))
    density = jnp.exp(-0.5 * preact * preact) * 0.3989422804014327
    return (preact * cumulative, cumulative + preact * density)


def contract_rows(left, right):
    return lax.dot_general(
        left, right, (((0,), (0,)), ((), ())), preferred_element_type=jnp.float32
    )


def contract_cols(left, right):
    return lax.dot_general(
        left, right, (((1,), (1,)), ((), ())), preferred_element_type=jnp.float32
    )


def adam_update(weights, grads, first, second, decay):
    new_first = beta_first * first + (1.0 - beta_first) * grads
    new_second = beta_second * second + (1.0 - beta_second) * grads * grads
    corr_first = 1.0 - beta_first**STEP
    corr_second = 1.0 - beta_second**STEP
    update = new_first / corr_first / (jnp.sqrt(new_second / corr_second) + adam_eps)
    new_weights = weights.astype(jnp.float32) * (1.0 - learn_rate * decay) - learn_rate * update
    return (new_weights, new_first, new_second)


def column_group(array, col_start, group_width, heads_in):
    return lax.dynamic_slice_in_dim(array, col_start, group_width, 1).reshape(
        array.shape[0], heads_in, HDIM
    )


def group_forward(queries, keys_all, values_all, valid_keys, group_width):
    row_count = queries.shape[0]
    heads_in = group_width // HDIM

    def one_group(group_index):
        col_start = group_index * group_width
        query_g = column_group(queries, col_start, group_width, heads_in)
        key_g = column_group(keys_all, col_start, group_width, heads_in)
        value_g = column_group(values_all, col_start, group_width, heads_in)
        scores = jnp.einsum("qhd,khd->hqk", query_g, key_g, preferred_element_type=jnp.float32)
        logsum = jnp.log(jnp.sum(jnp.where(valid_keys, jnp.exp(scores), 0.0), axis=2))
        attn_probs = jnp.where(valid_keys, jnp.exp(scores - logsum[:, :, None]), 0.0).astype(
            jnp.bfloat16
        )
        group_out = jnp.einsum(
            "hqk,khd->qhd", attn_probs, value_g, preferred_element_type=jnp.float32
        )
        return (group_out.reshape(row_count, group_width).astype(jnp.bfloat16), logsum)

    groups = queries.shape[1] // group_width
    group_outs, logsums = lax.map(one_group, jnp.arange(groups, dtype=jnp.int32))
    return (group_outs.transpose(1, 0, 2).reshape(row_count, groups * group_width), logsums)


def group_backward(
    queries, keys_all, values_all, mixed, grad_mixed, logsums, valid_keys, group_width
):
    row_count = queries.shape[0]
    key_count = keys_all.shape[0]
    heads_in = group_width // HDIM
    head_scale = HDIM ** (-0.5)

    def one_group(items):
        group_index, logsum = items
        col_start = group_index * group_width
        query_g = column_group(queries, col_start, group_width, heads_in)
        key_g = column_group(keys_all, col_start, group_width, heads_in)
        value_g = column_group(values_all, col_start, group_width, heads_in)
        mixed_g = column_group(mixed, col_start, group_width, heads_in)
        grad_g = column_group(grad_mixed, col_start, group_width, heads_in)
        scores = jnp.einsum("qhd,khd->hqk", query_g, key_g, preferred_element_type=jnp.float32)
        probs_full = jnp.where(valid_keys, jnp.exp(scores - logsum[:, :, None]), 0.0)
        probs_low = probs_full.astype(jnp.bfloat16)
        grad_probs = jnp.einsum("qhd,khd->hqk", grad_g, value_g, preferred_element_type=jnp.float32)
        row_delta = jnp.sum(grad_g.astype(jnp.float32) * mixed_g.astype(jnp.float32), axis=2).T
        grad_scores = (probs_full * (grad_probs - row_delta[:, :, None])).astype(jnp.bfloat16)
        grad_query = (
            jnp.einsum("hqk,khd->qhd", grad_scores, key_g, preferred_element_type=jnp.float32)
            * head_scale
        )
        grad_key = jnp.einsum(
            "hqk,qhd->khd", grad_scores, query_g, preferred_element_type=jnp.float32
        )
        grad_value = jnp.einsum(
            "hqk,qhd->khd", probs_low, grad_g, preferred_element_type=jnp.float32
        )
        return (
            grad_query.reshape(row_count, group_width),
            grad_key.reshape(key_count, group_width),
            grad_value.reshape(key_count, group_width),
        )

    groups = queries.shape[1] // group_width
    stacked = lax.map(one_group, (jnp.arange(groups, dtype=jnp.int32), logsums))
    return tuple(
        (
            piece.transpose(1, 0, 2).reshape(piece.shape[1], groups * group_width)
            for piece in stacked
        )
    )


CTX = ("a", "b")
EVERY = ("a", "b", "x", "c")


def shift(array, axis):
    count = lax.axis_size(axis)
    return lax.ppermute(array, axis, [(i, (i + 1) % count) for i in range(count)])


def place(whole, piece, position, dim):
    return lax.dynamic_update_index_in_dim(whole, piece, position, dim)


def ring_gather(piece, axis, dim):
    count, index = lax.axis_size(axis), lax.axis_index(axis)
    whole = jnp.zeros(piece.shape[:dim] + (count,) + piece.shape[dim:], piece.dtype)
    whole = place(whole, piece, index, dim)
    moving = piece
    for step in range(1, count):
        moving = shift(moving, axis)
        whole = place(whole, moving, lax.rem(index - step + count, count), dim)
    return whole


def gather_rows(rows, first):
    depth, columns = rows.shape
    lined = ring_gather(rows, "a", 0)
    left, right = lined[:, :, :first], lined[:, :, first:]
    left = ring_gather(ring_gather(left, "b", 1), "x", 2)
    right = ring_gather(ring_gather(right, "x", 1), "b", 1)
    left, right = ring_gather(left, "c", 3), ring_gather(right, "c", 3)
    return left.reshape(-1, first), right.reshape(-1, columns - first)


def ring_scatter(terms, axis, dim, last=jnp.bfloat16):
    count, index = lax.axis_size(axis), lax.axis_index(axis)

    def block(offset):
        return lax.dynamic_index_in_dim(terms, lax.rem(index + offset, count), dim, keepdims=False)

    total = block(count - 1)
    for step in range(1, count):
        kind = last if step == count - 1 else terms.dtype
        total = shift(total, axis).astype(jnp.float32) + block(2 * count - 1 - step).astype(jnp.float32)
        total = total.astype(kind)
    return total


def scatter_grads(left, right):
    count, width = left.shape
    cores, core = lax.axis_size("c"), lax.axis_index("c")
    chips = [lax.axis_size(axis) for axis in ("a", "b", "x")]
    depth = width // (cores * chips[0] * chips[1] * chips[2])
    blocks = left.reshape(count, -1, cores, depth)

    def term(offset):
        mine = lax.dynamic_index_in_dim(blocks, lax.rem(core + offset, cores), 2, keepdims=False)
        return contract_rows(mine.reshape(count, -1), right)

    total = term(cores - 1).astype(jnp.bfloat16)
    for step in range(1, cores):
        total = (shift(total, "c").astype(jnp.float32) + term(2 * cores - 1 - step)).astype(
            jnp.bfloat16
        )
    total = total.reshape(chips + [depth, -1])
    half = (total.shape[-1] // 256) * 128
    first = ring_scatter(ring_scatter(total[..., :half], "x", 2), "b", 1)
    second = ring_scatter(ring_scatter(total[..., half:], "b", 1), "x", 1)
    first = ring_scatter(first, "a", 0, jnp.float32)
    second = ring_scatter(second, "a", 0, jnp.float32)
    return jnp.concatenate([first, second], axis=1)


def attend_kernel(heads, length_ref, query_ref, key_ref, value_ref, mixed_ref, logsum_ref):
    query, key, value = query_ref[...], key_ref[...], value_ref[...]
    lanes = lax.broadcasted_iota(jnp.int32, (1, query.shape[1]), 1) // HDIM
    valid = lax.broadcasted_iota(jnp.int32, (1, key.shape[0]), 1) < length_ref[0]
    mixed = jnp.zeros(query.shape, jnp.float32)
    logsums = jnp.zeros(query.shape, jnp.float32)
    for head in range(heads):
        mine = lanes == head
        scores = contract_cols(jnp.where(mine, query, jnp.zeros_like(query)), key)
        total = jnp.sum(jnp.where(valid, jnp.exp(scores), 0.0), axis=1, keepdims=True)
        logsum = jnp.log(total)
        probs = jnp.where(valid, jnp.exp(scores - logsum), 0.0).astype(jnp.bfloat16)
        out = jnp.dot(probs, value, preferred_element_type=jnp.float32)
        mixed = jnp.where(mine, out, mixed)
        logsums = jnp.where(mine, logsum, logsums)
    mixed_ref[...] = mixed.astype(jnp.bfloat16)
    logsum_ref[...] = logsums


def attend_back_kernel(
    heads,
    length_ref,
    query_ref,
    key_ref,
    value_ref,
    mixed_ref,
    logsum_ref,
    grad_ref,
    out_ref,
    key_acc,
    value_acc,
):
    step = pl.program_id(0)
    rows, wide = query_ref.shape

    @pl.when(step == 0)
    def _():
        key_acc[...] = jnp.zeros_like(key_acc)
        value_acc[...] = jnp.zeros_like(value_acc)

    query, key, value = query_ref[...], key_ref[...], value_ref[...]
    grad, logsums = grad_ref[...], logsum_ref[...]
    lanes = lax.broadcasted_iota(jnp.int32, (1, wide), 1) // HDIM
    valid = lax.broadcasted_iota(jnp.int32, (1, key.shape[0]), 1) < length_ref[0]
    products = grad.astype(jnp.float32) * mixed_ref[...].astype(jnp.float32)
    grad_query = jnp.zeros(query.shape, jnp.float32)
    for head in range(heads):
        mine = lanes == head
        query_h = jnp.where(mine, query, jnp.zeros_like(query))
        grad_h = jnp.where(mine, grad, jnp.zeros_like(grad))
        logsum = logsums[:, head * HDIM : head * HDIM + 1]
        delta = jnp.sum(jnp.where(mine, products, 0.0), axis=1, keepdims=True)
        scores = contract_cols(query_h, key)
        probs = jnp.where(valid, jnp.exp(scores - logsum), 0.0)
        grad_probs = contract_cols(grad_h, value)
        grad_scores = (probs * (grad_probs - delta)).astype(jnp.bfloat16)
        out = jnp.dot(grad_scores, key, preferred_element_type=jnp.float32)
        grad_query = jnp.where(mine, out, grad_query)
        key_acc[...] += contract_rows(grad_scores, query_h)
        value_acc[...] += contract_rows(probs.astype(jnp.bfloat16), grad_h)
    start = pl.multiple_of(step * rows, rows)
    out_ref[pl.ds(start, rows), :wide] = (grad_query * HDIM ** (-0.5)).astype(jnp.bfloat16)

    @pl.when(step == pl.num_programs(0) - 1)
    def _():
        out_ref[:, wide : 2 * wide] = key_acc[...].astype(jnp.bfloat16)
        out_ref[:, 2 * wide :] = value_acc[...].astype(jnp.bfloat16)


def attend(packed, lengths):
    positions, wide = packed.shape[0], packed.shape[1] // 3
    block = min(256, positions)
    part = lambda which: pl.BlockSpec((positions, wide), lambda i, n: (0, which))
    rows = pl.BlockSpec((block, wide), lambda i, n: (i, 0))
    return pl.pallas_call(
        functools.partial(attend_kernel, wide // HDIM),
        grid_spec=pltpu.PrefetchScalarGridSpec(
            num_scalar_prefetch=1,
            grid=(positions // block,),
            in_specs=[rows, part(1), part(2)],
            out_specs=[rows, rows],
        ),
        out_shape=[
            jax.ShapeDtypeStruct((positions, wide), jnp.bfloat16),
            jax.ShapeDtypeStruct((positions, wide), jnp.float32),
        ],
        cost_estimate=pl.CostEstimate(
            flops=4 * positions * positions * wide,
            transcendentals=2 * positions * positions * wide // HDIM,
            bytes_accessed=12 * positions * wide,
        ),
    )(lengths, packed, packed, packed)


def attend_back(packed, lengths, mixed, logsums, grads):
    positions, wide = mixed.shape
    block = min(256, positions)
    part = lambda which: pl.BlockSpec((positions, wide), lambda i, n: (0, which))
    rows = pl.BlockSpec((block, wide), lambda i, n: (i, 0))
    return pl.pallas_call(
        functools.partial(attend_back_kernel, wide // HDIM),
        grid_spec=pltpu.PrefetchScalarGridSpec(
            num_scalar_prefetch=1,
            grid=(positions // block,),
            in_specs=[rows, part(1), part(2), rows, rows, rows],
            out_specs=pl.BlockSpec((positions, 3 * wide), lambda i, n: (0, 0)),
            scratch_shapes=[pltpu.VMEM((positions, wide), jnp.float32)] * 2,
        ),
        out_shape=jax.ShapeDtypeStruct((positions, 3 * wide), jnp.bfloat16),
        cost_estimate=pl.CostEstimate(
            flops=10 * positions * positions * wide,
            transcendentals=positions * positions * wide // HDIM,
            bytes_accessed=20 * positions * wide,
        ),
    )(lengths, packed, packed, packed, mixed, logsums, grads)


def to_heads(rows, kinds):
    groups = lax.axis_size(CTX)
    count, width = rows.shape
    wide = width // (kinds * groups)
    cut = rows.reshape(count, kinds, groups, wide).transpose(2, 0, 1, 3)
    cut = cut.reshape(groups, count, kinds * wide)
    moved = lax.all_to_all(cut, CTX, 0, 0, tiled=True)
    return moved.reshape(groups * count, kinds * wide)


def to_positions(rows, kinds):
    groups = lax.axis_size(CTX)
    count, wide = rows.shape[0] // groups, rows.shape[1] // kinds
    moved = lax.all_to_all(rows.reshape(groups, count, kinds * wide), CTX, 0, 0, tiled=True)
    moved = moved.reshape(groups, count, kinds, wide).transpose(1, 2, 0, 3)
    return moved.reshape(count, kinds * groups * wide)


def local(
    tokens,
    cotangent,
    lengths,
    matrices,
    vectors,
    first_moment,
    second_moment,
    vec_first,
    vec_second,
):
    inputs = tokens[0]
    upstream = cotangent[0]
    length = lengths[0]
    width = inputs.shape[1]
    group_width = min(width, 256)
    head_scale = HDIM ** (-0.5)
    hidden_width = (matrices.shape[1] - 4 * width) // 2
    vector_count = vectors.shape[0]
    extra = -vector_count % 128
    head = jnp.concatenate(
        [matrices[:, : 3 * width], jnp.pad(vectors.T, ((0, 0), (0, extra)))], axis=1
    )
    qkv_first = (3 * width // 256) * 128
    qkv_left, qkv_right = gather_rows(head, qkv_first)
    qkv_rest = 3 * width - qkv_first
    vector_rows = qkv_right[:, qkv_rest : qkv_rest + vector_count].T.astype(jnp.float32)
    qkv_right = qkv_right[:, :qkv_rest]
    full_rest = lax.all_gather(matrices[:, 3 * width :], EVERY, axis=0, tiled=True)
    weight_out = full_rest[:, :width]
    weight_up = full_rest[:, width : width + hidden_width]
    weight_down = full_rest[:, width + hidden_width :]
    bias_up = vector_rows[8:].reshape(-1)
    projected = jnp.concatenate(
        [
            jnp.dot(inputs, qkv_left, preferred_element_type=jnp.float32),
            jnp.dot(inputs, qkv_right, preferred_element_type=jnp.float32),
        ],
        axis=1,
    )
    queries = ((projected[:, :width] + vector_rows[0]) * head_scale).astype(jnp.bfloat16)
    keys_own = projected[:, width : 2 * width].astype(jnp.bfloat16)
    values_own = (projected[:, 2 * width :] + vector_rows[1]).astype(jnp.bfloat16)
    groups = lax.axis_size(CTX)
    by_heads = width % (groups * 128) == 0
    if by_heads:
        packed = to_heads(jnp.concatenate([queries, keys_own, values_own], axis=1), 3)
        mixed_heads, logsums = attend(packed, lengths)
        mixed = to_positions(mixed_heads, 1)
    else:
        keys_all, values_all = (
            lax.all_gather(keys_own, CTX, axis=0, tiled=True),
            lax.all_gather(values_own, CTX, axis=0, tiled=True),
        )
        valid_keys = jnp.arange(keys_all.shape[0], dtype=jnp.int32) < length
        mixed, logsums = group_forward(queries, keys_all, values_all, valid_keys, group_width)
    resid_one = (
        inputs.astype(jnp.float32)
        + jnp.dot(mixed, weight_out, preferred_element_type=jnp.float32)
        + vector_rows[2]
    )
    hidden, normed_one, inverse_one = norm_forward(resid_one, vector_rows[3], vector_rows[4])
    hidden_low = hidden.astype(jnp.bfloat16)
    preact = jnp.dot(hidden_low, weight_up, preferred_element_type=jnp.float32) + bias_up
    activ_full, gelu_slope = gelu_parts(preact)
    activated = activ_full.astype(jnp.bfloat16)
    resid_two = hidden + contract_cols(activated, weight_down) + vector_rows[5]
    outputs, normed_two, inverse_two = norm_forward(resid_two, vector_rows[6], vector_rows[7])
    grad_resid_two = norm_backward(upstream, vector_rows[6], normed_two, inverse_two)
    grad_two_low = grad_resid_two.astype(jnp.bfloat16)
    grad_down = scatter_grads(grad_two_low, activated)
    grad_preact = jnp.dot(grad_two_low, weight_down, preferred_element_type=jnp.float32) * gelu_slope
    grad_preact_low = grad_preact.astype(jnp.bfloat16)
    grad_up = scatter_grads(hidden_low, grad_preact_low)
    grad_hidden = grad_resid_two + contract_cols(grad_preact_low, weight_up)
    grad_resid_one = norm_backward(grad_hidden, vector_rows[3], normed_one, inverse_one)
    grad_one_low = grad_resid_one.astype(jnp.bfloat16)
    grad_out = scatter_grads(mixed, grad_one_low)
    grad_mixed = contract_cols(grad_one_low, weight_out).astype(jnp.bfloat16)
    if by_heads:
        grad_heads = attend_back(packed, lengths, mixed_heads, logsums, to_heads(grad_mixed, 1))
        grad_proj = to_positions(grad_heads, 3)
        grad_query = grad_proj[:, :width].astype(jnp.float32)
        grad_value = grad_proj[:, 2 * width :].astype(jnp.float32)
    else:
        grad_query, key_terms, value_terms = group_backward(
            queries, keys_all, values_all, mixed, grad_mixed, logsums, valid_keys, group_width
        )
        grad_key, grad_value = (
            lax.psum_scatter(
                terms.astype(jnp.bfloat16), CTX, scatter_dimension=0, tiled=True
            ).astype(jnp.float32)
            for terms in (key_terms, value_terms)
        )
        grad_proj = jnp.concatenate([grad_query, grad_key, grad_value], axis=1).astype(jnp.bfloat16)
    grad_qkv = scatter_grads(inputs, grad_proj)
    grad_input = (
        grad_resid_one
        + contract_cols(grad_proj[:, :qkv_first], qkv_left)
        + contract_cols(grad_proj[:, qkv_first:], qkv_right)
    )
    small_rows = jnp.stack(
        [
            jnp.sum(grad_query, axis=0),
            jnp.sum(grad_value, axis=0),
            jnp.sum(grad_resid_one, axis=0),
            jnp.sum(grad_hidden * normed_one, axis=0),
            jnp.sum(grad_hidden, axis=0),
            jnp.sum(grad_resid_two, axis=0),
            jnp.sum(upstream * normed_two, axis=0),
            jnp.sum(upstream, axis=0),
        ]
    )
    vec_term = jnp.concatenate(
        [small_rows, jnp.sum(grad_preact, axis=0).reshape(-1, width)], axis=0
    )
    sizes = [lax.axis_size(axis) for axis in EVERY]
    vec_blocks = vec_term.reshape([vector_count] + sizes + [-1])
    for dim, axis in ((4, "c"), (3, "x"), (2, "b"), (1, "a")):
        vec_blocks = ring_scatter(vec_blocks, axis, dim, jnp.float32)
    grad_vectors = vec_blocks
    grad_matrices = jnp.concatenate([grad_qkv, grad_out, grad_up, grad_down], axis=1)
    new_matrices, new_first, new_second = adam_update(
        matrices, grad_matrices, first_moment, second_moment, decay_rate
    )
    new_vectors, new_vec_first, new_vec_second = adam_update(
        vectors, grad_vectors, vec_first, vec_second, 0.0
    )
    return (
        outputs[None],
        grad_input[None],
        grad_matrices,
        grad_vectors,
        new_matrices,
        new_vectors,
        new_first,
        new_second,
        new_vec_first,
        new_vec_second,
    )


def solution(mesh):
    ctx, shard = mesh.shape["ctx"], mesh.shape["shard"]
    mesh = Mesh(mesh.devices.reshape(ctx // 2, 2, shard // 2, 2), EVERY)
    placed = (
        P(("x", "c"), CTX, None),
        P(("x", "c"), CTX, None),
        P(("x", "c")),
        P(EVERY, None),
        P(None, EVERY),
        P(EVERY, None),
        P(EVERY, None),
        P(None, EVERY),
        P(None, EVERY),
    )
    return jax.shard_map(
        local,
        mesh=mesh,
        in_specs=placed,
        out_specs=(
            P(("x", "c"), CTX, None),
            P(("x", "c"), CTX, None),
            P(EVERY, None),
            P(None, EVERY),
            P(EVERY, None),
            P(None, EVERY),
            P(EVERY, None),
            P(EVERY, None),
            P(None, EVERY),
            P(None, EVERY),
        ),
        check_vma=False,
    )
```

```python
import functools

import jax
import jax.numpy as jnp
from jax import lax
from jax.experimental import pallas as pl
from jax.experimental.pallas import tpu as pltpu
from jax.sharding import Mesh, PartitionSpec as P


HDIM = 64
STEP = 5


beta_first = 0.9
beta_second = 0.999
learn_rate = 0.02
decay_rate = 0.01
adam_eps = 1e-08
norm_eps = 1e-06


def norm_forward(resid, gain_row, shift_row):
    centered = resid - jnp.mean(resid, axis=-1, keepdims=True)
    inverse = lax.rsqrt(jnp.mean(centered * centered, axis=-1, keepdims=True) + norm_eps)
    normed = centered * inverse
    return (normed * gain_row + shift_row, normed, inverse)


def norm_backward(upstream, gain_row, normed, inverse):
    scaled = upstream * gain_row
    return inverse * (
        scaled
        - jnp.mean(scaled, axis=-1, keepdims=True)
        - normed * jnp.mean(scaled * normed, axis=-1, keepdims=True)
    )


def gelu_parts(preact):
    cumulative = 0.5 * (1.0 + lax.erf(preact * 0.7071067811865476))
    density = jnp.exp(-0.5 * preact * preact) * 0.3989422804014327
    return (preact * cumulative, cumulative + preact * density)


def contract_rows(left, right):
    return lax.dot_general(
        left, right, (((0,), (0,)), ((), ())), preferred_element_type=jnp.float32
    )


def contract_cols(left, right):
    return lax.dot_general(
        left, right, (((1,), (1,)), ((), ())), preferred_element_type=jnp.float32
    )


def adam_update(weights, grads, first, second, decay):
    new_first = beta_first * first + (1.0 - beta_first) * grads
    new_second = beta_second * second + (1.0 - beta_second) * grads * grads
    corr_first = 1.0 - beta_first**STEP
    corr_second = 1.0 - beta_second**STEP
    update = new_first / corr_first / (jnp.sqrt(new_second / corr_second) + adam_eps)
    new_weights = weights.astype(jnp.float32) * (1.0 - learn_rate * decay) - learn_rate * update
    return (new_weights, new_first, new_second)


def column_group(array, col_start, group_width, heads_in):
    return lax.dynamic_slice_in_dim(array, col_start, group_width, 1).reshape(
        array.shape[0], heads_in, HDIM
    )


def group_forward(queries, keys_all, values_all, valid_keys, group_width):
    row_count = queries.shape[0]
    heads_in = group_width // HDIM

    def one_group(group_index):
        col_start = group_index * group_width
        query_g = column_group(queries, col_start, group_width, heads_in)
        key_g = column_group(keys_all, col_start, group_width, heads_in)
        value_g = column_group(values_all, col_start, group_width, heads_in)
        scores = jnp.einsum("qhd,khd->hqk", query_g, key_g, preferred_element_type=jnp.float32)
        logsum = jnp.log(jnp.sum(jnp.where(valid_keys, jnp.exp(scores), 0.0), axis=2))
        attn_probs = jnp.where(valid_keys, jnp.exp(scores - logsum[:, :, None]), 0.0).astype(
            jnp.bfloat16
        )
        group_out = jnp.einsum(
            "hqk,khd->qhd", attn_probs, value_g, preferred_element_type=jnp.float32
        )
        return (group_out.reshape(row_count, group_width).astype(jnp.bfloat16), logsum)

    groups = queries.shape[1] // group_width
    group_outs, logsums = lax.map(one_group, jnp.arange(groups, dtype=jnp.int32))
    return (group_outs.transpose(1, 0, 2).reshape(row_count, groups * group_width), logsums)


def group_backward(
    queries, keys_all, values_all, mixed, grad_mixed, logsums, valid_keys, group_width
):
    row_count = queries.shape[0]
    key_count = keys_all.shape[0]
    heads_in = group_width // HDIM
    head_scale = HDIM ** (-0.5)

    def one_group(items):
        group_index, logsum = items
        col_start = group_index * group_width
        query_g = column_group(queries, col_start, group_width, heads_in)
        key_g = column_group(keys_all, col_start, group_width, heads_in)
        value_g = column_group(values_all, col_start, group_width, heads_in)
        mixed_g = column_group(mixed, col_start, group_width, heads_in)
        grad_g = column_group(grad_mixed, col_start, group_width, heads_in)
        scores = jnp.einsum("qhd,khd->hqk", query_g, key_g, preferred_element_type=jnp.float32)
        probs_full = jnp.where(valid_keys, jnp.exp(scores - logsum[:, :, None]), 0.0)
        probs_low = probs_full.astype(jnp.bfloat16)
        grad_probs = jnp.einsum("qhd,khd->hqk", grad_g, value_g, preferred_element_type=jnp.float32)
        row_delta = jnp.sum(grad_g.astype(jnp.float32) * mixed_g.astype(jnp.float32), axis=2).T
        grad_scores = (probs_full * (grad_probs - row_delta[:, :, None])).astype(jnp.bfloat16)
        grad_query = (
            jnp.einsum("hqk,khd->qhd", grad_scores, key_g, preferred_element_type=jnp.float32)
            * head_scale
        )
        grad_key = jnp.einsum(
            "hqk,qhd->khd", grad_scores, query_g, preferred_element_type=jnp.float32
        )
        grad_value = jnp.einsum(
            "hqk,qhd->khd", probs_low, grad_g, preferred_element_type=jnp.float32
        )
        return (
            grad_query.reshape(row_count, group_width),
            grad_key.reshape(key_count, group_width),
            grad_value.reshape(key_count, group_width),
        )

    groups = queries.shape[1] // group_width
    stacked = lax.map(one_group, (jnp.arange(groups, dtype=jnp.int32), logsums))
    return tuple(
        (
            piece.transpose(1, 0, 2).reshape(piece.shape[1], groups * group_width)
            for piece in stacked
        )
    )


CTX = ("a", "b")
EVERY = ("a", "b", "x", "c")


def shift(array, axis, by=1):
    count = lax.axis_size(axis)
    return lax.ppermute(array, axis, [(i, (i + by) % count) for i in range(count)])


class Line:
    def __init__(self):
        self.last = None

    def tie(self, *arrays):
        if self.last is None:
            return arrays if len(arrays) > 1 else arrays[0]
        tied = lax.optimization_barrier(arrays + (self.last,))[:-1]
        return tied if len(arrays) > 1 else tied[0]

    def mark(self, array):
        self.last = array
        return array


class Chain:
    def __init__(self, line, steps):
        self.line, self.steps, self.value = line, steps, None
        next(steps)

    def step(self):
        try:
            next(self.steps)
        except StopIteration as stop:
            self.value = stop.value
        return self


def pair_gather(line, piece, axis, dim):
    moved = shift(piece, axis)
    yield
    moved = line.tie(moved)
    first = lax.axis_index(axis) == 0
    both = [jnp.where(first, piece, moved), jnp.where(first, moved, piece)]
    return line.mark(jnp.stack(both, axis=dim))


def spread(piece, axes):
    copies = jnp.broadcast_to(piece, (lax.axis_size(axes),) + piece.shape)
    return lax.all_to_all(copies, axes, 0, 0, tiled=True)


def stage_scatter(line, jobs):
    moved, kept = [], []
    for terms, axis, dim, _ in jobs:
        count, index = lax.axis_size(axis), lax.axis_index(axis)
        cut = [
            lax.dynamic_index_in_dim(terms, lax.rem(index + s, count), dim, keepdims=False)
            for s in range(count)
        ]
        moved.append([shift(cut[s], axis, s) for s in range(1, count)])
        kept.append(cut[0])
    yield
    results = []
    for (_, _, _, kind), parts, own in zip(jobs, moved, kept):
        parts = line.tie(*parts) if len(parts) > 1 else [line.tie(parts[0])]
        total = sum((p.astype(jnp.float32) for p in parts), own.astype(jnp.float32))
        results.append(total.astype(kind))
    line.mark(results[-1])
    return results


def token_rows(line, rows):
    count, index = lax.axis_size("a"), lax.axis_index("a")
    moved = [rows] + [shift(rows, "a", step) for step in range(1, count)]
    yield
    lined = jnp.zeros((count,) + rows.shape, rows.dtype)
    for step, part in enumerate(line.tie(*moved)):
        place = lax.rem(index - step + count, count)
        lined = lax.dynamic_update_index_in_dim(lined, part, place, 0)
    lined = yield from pair_gather(line, line.mark(lined), "b", 1)
    return lined.reshape(-1, rows.shape[1])


def all_rows(rows):
    return lax.all_gather(rows, EVERY, axis=0, tiled=True)


def scatter_steps(line, terms, stages):
    for axis, dim, kind in stages:
        (terms,) = yield from stage_scatter(line, [(terms, axis, dim, kind)])
    return terms


def reordered(left):
    width = left.shape[1]
    sizes = [lax.axis_size(axis) for axis in EVERY]
    lines = sizes[0]
    depth = width // (8 * lines)
    a_, b_, x_, c_ = (lax.axis_index(axis) for axis in EVERY)
    column = lax.broadcasted_iota(jnp.int32, (width, 2 * width), 1)
    row = lax.broadcasted_iota(jnp.int32, (width, 2 * width), 0)
    swapped = column >= width
    column = lax.rem(column, width)
    low, block = lax.rem(column, depth), column // depth
    place, block = lax.rem(block, lines), block // lines
    inner, outer, core = lax.rem(block, 2), lax.rem(block // 2, 2), block // 4
    along_x, along_b = jnp.where(swapped, inner, outer), jnp.where(swapped, outer, inner)
    owner = lax.rem(place + a_, lines) * 8 + lax.rem(along_b + b_, 2) * 4 + lax.rem(along_x + x_, 2) * 2
    owner = owner + lax.rem(core + c_, 2)
    return (row == owner * depth + low).astype(jnp.bfloat16)


def scatter_grads(line, left, right, order):
    width = left.shape[1]
    depth = width // lax.axis_size(EVERY)
    left = jnp.dot(left, order, preferred_element_type=jnp.float32).astype(jnp.bfloat16)
    half = right.shape[1] // 256 * 128
    sides = ((left[:, :width], right[:, :half]), (left[:, width:], right[:, half:]))
    axes = (("c", "x", "b"), ("c", "b", "x"))
    got = [[], []]
    size = width
    for stage in range(3):
        size //= 2
        sent = []
        for side, (rows, columns) in enumerate(sides):
            term = contract_rows(rows[:, size : 2 * size], columns)
            for part in got[side]:
                term = term + part[size : 2 * size].astype(jnp.float32)
            sent.append(shift(term.astype(jnp.bfloat16), axes[side][stage]))
        yield
        sent = line.tie(*sent)
        for side in range(2):
            got[side].append(sent[side])
        line.mark(sent[0])
    lines = []
    for side, (rows, columns) in enumerate(sides):
        term = contract_rows(rows[:, :size], columns)
        for part in got[side]:
            term = term + part[:size].astype(jnp.float32)
        lines.append(term.astype(jnp.bfloat16))
    lines = jnp.concatenate(lines, axis=1).reshape(-1, depth, right.shape[1])
    moved = [shift(lines[step], "a", step) for step in range(1, lines.shape[0])]
    yield
    moved = line.tie(*moved)
    total = sum((part.astype(jnp.float32) for part in moved), lines[0].astype(jnp.float32))
    return line.mark(total)


def moved_to_heads(line, array):
    moved = lax.all_to_all(array, CTX, 0, 0, tiled=True)
    yield
    return line.mark(line.tie(moved))


def heads_weights(line, rows, vectors, groups, wide):
    depth = rows.shape[0]
    cut = rows.reshape(depth, 3, groups, wide).transpose(2, 0, 1, 3)
    cut = cut.reshape(groups, depth, 3 * wide)
    beside = jnp.pad(vectors.T, ((0, 0), (0, -vectors.shape[0] % 128)))
    beside = jnp.broadcast_to(beside, (groups,) + beside.shape)
    moved = yield from moved_to_heads(line, jnp.concatenate([cut, beside], axis=2))
    moved = yield from pair_gather(line, moved, "x", 1)
    moved = yield from pair_gather(line, moved, "c", 2)
    moved = moved.reshape(-1, moved.shape[-1])
    return moved[:, : 3 * wide], moved[:, 3 * wide : 3 * wide + vectors.shape[0]].T


def heads_grads(line, terms, vectors, groups, wide):
    count = vectors.shape[0]
    beside = jnp.pad(vectors.T, ((0, 0), (0, -count % 128))).astype(jnp.bfloat16)
    terms = jnp.concatenate([terms, beside], axis=1)
    sizes = [groups, lax.axis_size("x"), lax.axis_size("c"), -1, terms.shape[1]]
    low = jnp.bfloat16
    terms = yield from scatter_steps(line, terms.reshape(sizes), (("c", 2, low), ("x", 1, low)))
    moved = yield from moved_to_heads(line, terms)
    beside = moved[:, :, 3 * wide : 3 * wide + count].astype(jnp.float32)
    moved = moved[:, :, : 3 * wide].reshape(groups, -1, 3, wide).transpose(1, 2, 0, 3)
    moved = moved.reshape(-1, 3 * groups * wide).astype(jnp.float32)
    return moved, jnp.sum(beside, axis=0).T


def attend_kernel(heads, length_ref, query_ref, key_ref, value_ref, mixed_ref, logsum_ref):
    query, key, value = query_ref[...], key_ref[...], value_ref[...]
    lanes = lax.broadcasted_iota(jnp.int32, (1, query.shape[1]), 1) // HDIM
    valid = lax.broadcasted_iota(jnp.int32, (1, key.shape[0]), 1) < length_ref[0]
    mixed = jnp.zeros(query.shape, jnp.float32)
    logsums = jnp.zeros(query.shape, jnp.float32)
    for head in range(heads):
        mine = lanes == head
        scores = contract_cols(jnp.where(mine, query, jnp.zeros_like(query)), key)
        total = jnp.sum(jnp.where(valid, jnp.exp(scores), 0.0), axis=1, keepdims=True)
        logsum = jnp.log(total)
        probs = jnp.where(valid, jnp.exp(scores - logsum), 0.0).astype(jnp.bfloat16)
        out = jnp.dot(probs, value, preferred_element_type=jnp.float32)
        mixed = jnp.where(mine, out, mixed)
        logsums = jnp.where(mine, logsum, logsums)
    mixed_ref[...] = mixed.astype(jnp.bfloat16)
    logsum_ref[...] = logsums


def attend_back_kernel(
    heads,
    length_ref,
    query_ref,
    key_ref,
    value_ref,
    mixed_ref,
    logsum_ref,
    grad_ref,
    out_ref,
    key_acc,
    value_acc,
):
    step = pl.program_id(0)
    rows, wide = query_ref.shape

    @pl.when(step == 0)
    def _():
        key_acc[...] = jnp.zeros_like(key_acc)
        value_acc[...] = jnp.zeros_like(value_acc)

    query, key, value = query_ref[...], key_ref[...], value_ref[...]
    grad, logsums = grad_ref[...], logsum_ref[...]
    lanes = lax.broadcasted_iota(jnp.int32, (1, wide), 1) // HDIM
    valid = lax.broadcasted_iota(jnp.int32, (1, key.shape[0]), 1) < length_ref[0]
    products = grad.astype(jnp.float32) * mixed_ref[...].astype(jnp.float32)
    grad_query = jnp.zeros(query.shape, jnp.float32)
    for head in range(heads):
        mine = lanes == head
        query_h = jnp.where(mine, query, jnp.zeros_like(query))
        grad_h = jnp.where(mine, grad, jnp.zeros_like(grad))
        logsum = logsums[:, head * HDIM : head * HDIM + 1]
        delta = jnp.sum(jnp.where(mine, products, 0.0), axis=1, keepdims=True)
        scores = contract_cols(query_h, key)
        probs = jnp.where(valid, jnp.exp(scores - logsum), 0.0)
        grad_probs = contract_cols(grad_h, value)
        grad_scores = (probs * (grad_probs - delta)).astype(jnp.bfloat16)
        out = jnp.dot(grad_scores, key, preferred_element_type=jnp.float32)
        grad_query = jnp.where(mine, out, grad_query)
        key_acc[...] += contract_rows(grad_scores, query_h)
        value_acc[...] += contract_rows(probs.astype(jnp.bfloat16), grad_h)
    start = pl.multiple_of(step * rows, rows)
    out_ref[pl.ds(start, rows), :wide] = (grad_query * HDIM ** (-0.5)).astype(jnp.bfloat16)

    @pl.when(step == pl.num_programs(0) - 1)
    def _():
        out_ref[:, wide : 2 * wide] = key_acc[...].astype(jnp.bfloat16)
        out_ref[:, 2 * wide :] = value_acc[...].astype(jnp.bfloat16)


def attend(packed, lengths):
    positions, wide = packed.shape[0], packed.shape[1] // 3
    block = min(256, positions)
    part = lambda which: pl.BlockSpec((positions, wide), lambda i, n: (0, which))
    rows = pl.BlockSpec((block, wide), lambda i, n: (i, 0))
    return pl.pallas_call(
        functools.partial(attend_kernel, wide // HDIM),
        grid_spec=pltpu.PrefetchScalarGridSpec(
            num_scalar_prefetch=1,
            grid=(positions // block,),
            in_specs=[rows, part(1), part(2)],
            out_specs=[rows, rows],
        ),
        out_shape=[
            jax.ShapeDtypeStruct((positions, wide), jnp.bfloat16),
            jax.ShapeDtypeStruct((positions, wide), jnp.float32),
        ],
        cost_estimate=pl.CostEstimate(
            flops=4 * positions * positions * wide,
            transcendentals=2 * positions * positions * wide // HDIM,
            bytes_accessed=12 * positions * wide,
        ),
    )(lengths, packed, packed, packed)


def attend_back(packed, lengths, mixed, logsums, grads):
    positions, wide = mixed.shape
    block = min(256, positions)
    part = lambda which: pl.BlockSpec((positions, wide), lambda i, n: (0, which))
    rows = pl.BlockSpec((block, wide), lambda i, n: (i, 0))
    return pl.pallas_call(
        functools.partial(attend_back_kernel, wide // HDIM),
        grid_spec=pltpu.PrefetchScalarGridSpec(
            num_scalar_prefetch=1,
            grid=(positions // block,),
            in_specs=[rows, part(1), part(2), rows, rows, rows],
            out_specs=pl.BlockSpec((positions, 3 * wide), lambda i, n: (0, 0)),
            scratch_shapes=[pltpu.VMEM((positions, wide), jnp.float32)] * 2,
        ),
        out_shape=jax.ShapeDtypeStruct((positions, 3 * wide), jnp.bfloat16),
        cost_estimate=pl.CostEstimate(
            flops=10 * positions * positions * wide,
            transcendentals=positions * positions * wide // HDIM,
            bytes_accessed=20 * positions * wide,
        ),
    )(lengths, packed, packed, packed, mixed, logsums, grads)


def to_heads(rows, kinds):
    groups = lax.axis_size(CTX)
    count, width = rows.shape
    wide = width // (kinds * groups)
    cut = rows.reshape(count, kinds, groups, wide).transpose(2, 0, 1, 3)
    cut = cut.reshape(groups, count, kinds * wide)
    moved = lax.all_to_all(cut, CTX, 0, 0, tiled=True)
    return moved.reshape(groups * count, kinds * wide)


def to_positions(rows, kinds):
    groups = lax.axis_size(CTX)
    count, wide = rows.shape[0] // groups, rows.shape[1] // kinds
    moved = lax.all_to_all(rows.reshape(groups, count, kinds * wide), CTX, 0, 0, tiled=True)
    moved = moved.reshape(groups, count, kinds, wide).transpose(1, 2, 0, 3)
    return moved.reshape(count, kinds * groups * wide)


def local(
    tokens,
    cotangent,
    lengths,
    matrices,
    vectors,
    first_moment,
    second_moment,
    vec_first,
    vec_second,
):
    inputs = tokens[0]
    upstream = cotangent[0]
    length = lengths[0]
    width = inputs.shape[1]
    group_width = min(width, 256)
    head_scale = HDIM ** (-0.5)
    hidden_width = (matrices.shape[1] - 4 * width) // 2
    vector_count = vectors.shape[0]
    groups = lax.axis_size(CTX)
    wide = width // groups
    by_heads = width % (groups * 128) == 0
    rows_qkv = matrices[:, : 3 * width]
    line = Line()
    chain = lambda make, *args: Chain(line, make(line, *args))
    full_rest = all_rows(matrices[:, 3 * width :])
    weight_out = full_rest[:, :width]
    weight_up = full_rest[:, width : width + hidden_width]
    weight_down = full_rest[:, width + hidden_width :]
    if by_heads:
        heads_chain = chain(heads_weights, rows_qkv, vectors, groups, wide)
        left_chain = chain(token_rows, inputs[:, : width // 2])
        right_chain = chain(token_rows, inputs[:, width // 2 :])
        left_chain.step()
        heads_chain.step()
        right_chain.step()
        heads_chain.step()
        tokens_left = left_chain.step().value
        weight_heads, vector_rows = heads_chain.step().value
        vector_rows = vector_rows.astype(jnp.float32)
        tokens_right = right_chain.step().value
        projected = jnp.dot(
            tokens_left, weight_heads[: width // 2], preferred_element_type=jnp.float32
        ) + jnp.dot(tokens_right, weight_heads[width // 2 :], preferred_element_type=jnp.float32)
        own = lax.dynamic_slice_in_dim(vector_rows, lax.axis_index(CTX) * wide, wide, 1)
        packed = jnp.concatenate(
            [
                (projected[:, :wide] + own[0]) * head_scale,
                projected[:, wide : 2 * wide],
                projected[:, 2 * wide :] + own[1],
            ],
            axis=1,
        ).astype(jnp.bfloat16)
        mixed_heads, logsums = attend(packed, lengths)
        mixed = to_positions(mixed_heads, 1)
    else:
        vector_rows = spread(vectors.T, EVERY).reshape(width, vector_count).T.astype(jnp.float32)
        weight_qkv = all_rows(rows_qkv)
        projected = jnp.dot(inputs, weight_qkv, preferred_element_type=jnp.float32)
        queries = ((projected[:, :width] + vector_rows[0]) * head_scale).astype(jnp.bfloat16)
        keys_own = projected[:, width : 2 * width].astype(jnp.bfloat16)
        values_own = (projected[:, 2 * width :] + vector_rows[1]).astype(jnp.bfloat16)
        keys_all, values_all = (
            lax.all_gather(keys_own, CTX, axis=0, tiled=True),
            lax.all_gather(values_own, CTX, axis=0, tiled=True),
        )
        valid_keys = jnp.arange(keys_all.shape[0], dtype=jnp.int32) < length
        mixed, logsums = group_forward(queries, keys_all, values_all, valid_keys, group_width)
    bias_up = vector_rows[8:].reshape(-1)
    resid_one = (
        inputs.astype(jnp.float32)
        + jnp.dot(mixed, weight_out, preferred_element_type=jnp.float32)
        + vector_rows[2]
    )
    hidden, normed_one, inverse_one = norm_forward(resid_one, vector_rows[3], vector_rows[4])
    hidden_low = hidden.astype(jnp.bfloat16)
    preact = jnp.dot(hidden_low, weight_up, preferred_element_type=jnp.float32) + bias_up
    activ_full, gelu_slope = gelu_parts(preact)
    activated = activ_full.astype(jnp.bfloat16)
    resid_two = hidden + contract_cols(activated, weight_down) + vector_rows[5]
    outputs, normed_two, inverse_two = norm_forward(resid_two, vector_rows[6], vector_rows[7])
    grad_resid_two = norm_backward(upstream, vector_rows[6], normed_two, inverse_two)
    grad_two_low = grad_resid_two.astype(jnp.bfloat16)
    if by_heads:
        weight_qkv = all_rows(lax.optimization_barrier((rows_qkv, resid_one))[0])
    order = reordered(inputs)
    line.mark(grad_two_low)
    down_grads = chain(scatter_grads, grad_two_low, activated, order)
    grad_preact = jnp.dot(grad_two_low, weight_down, preferred_element_type=jnp.float32) * gelu_slope
    grad_preact_low = line.mark(grad_preact.astype(jnp.bfloat16))
    up_grads = chain(scatter_grads, hidden_low, grad_preact_low, order)
    down_grads.step()
    grad_hidden = grad_resid_two + contract_cols(line.tie(grad_preact_low), weight_up)
    grad_resid_one = norm_backward(grad_hidden, vector_rows[3], normed_one, inverse_one)
    grad_one_low = grad_resid_one.astype(jnp.bfloat16)
    grad_mixed = contract_cols(grad_one_low, weight_out).astype(jnp.bfloat16)
    line.mark(grad_mixed)
    def vector_terms(query_sum, value_sum):
        small_rows = jnp.stack(
            [
                query_sum,
                value_sum,
                jnp.sum(grad_resid_one, axis=0),
                jnp.sum(grad_hidden * normed_one, axis=0),
                jnp.sum(grad_hidden, axis=0),
                jnp.sum(grad_resid_two, axis=0),
                jnp.sum(upstream * normed_two, axis=0),
                jnp.sum(upstream, axis=0),
            ]
        )
        return jnp.concatenate(
            [small_rows, jnp.sum(grad_preact, axis=0).reshape(-1, width)], axis=0
        )

    if by_heads:
        grad_all = to_heads(grad_mixed, 1)
        out_grads = chain(scatter_grads, mixed, grad_one_low, order)
        up_grads.step()
        down_grads.step()
        out_grads.step()
        grad_heads = attend_back(packed, lengths, mixed_heads, logsums, line.tie(grad_all))
        line.mark(grad_heads)
        grad_proj = to_positions(grad_heads, 3)
        sums = jnp.sum(grad_heads.astype(jnp.float32), axis=0).reshape(3, wide)
        all_sums = jnp.zeros((3, groups, wide), jnp.float32)
        all_sums = lax.dynamic_update_index_in_dim(all_sums, sums, lax.axis_index(CTX), 1)
        all_sums = all_sums.reshape(3, width)
        query_sum, value_sum = all_sums[0], all_sums[2]
        grad_cols = jnp.concatenate(
            [contract_rows(tokens_left, grad_heads), contract_rows(tokens_right, grad_heads)]
        ).astype(jnp.bfloat16)
        heads_chain = chain(
            heads_grads, grad_cols, vector_terms(query_sum, value_sum), groups, wide
        )
        up_grads.step()
        heads_chain.step()
        down_grads.step()
        heads_chain.step()
        out_grads.step()
        up_grads.step()
        out_grads.step()
    else:
        up_grads.step()
        out_grads = chain(scatter_grads, mixed, grad_one_low, order)
        for made in (down_grads, up_grads) * 2 + (out_grads,) * 3:
            made.step()
        grad_query, key_terms, value_terms = group_backward(
            queries, keys_all, values_all, mixed, grad_mixed, logsums, valid_keys, group_width
        )
        grad_key, grad_value = (
            lax.psum_scatter(
                terms.astype(jnp.bfloat16), CTX, scatter_dimension=0, tiled=True
            ).astype(jnp.float32)
            for terms in (key_terms, value_terms)
        )
        grad_proj = jnp.concatenate([grad_query, grad_key, grad_value], axis=1).astype(jnp.bfloat16)
        query_sum, value_sum = jnp.sum(grad_query, axis=0), jnp.sum(grad_value, axis=0)
        qkv_grads = chain(scatter_grads, inputs, grad_proj, order)
        for _ in range(3):
            qkv_grads.step()
    grad_input = grad_resid_one + contract_cols(grad_proj, weight_qkv)
    if by_heads:
        grad_qkv, grad_vectors = heads_chain.step().value
    else:
        grad_qkv = qkv_grads.step().value
        vec_blocks = vector_terms(query_sum, value_sum)
        vec_blocks = vec_blocks.reshape(vector_count, lax.axis_size(EVERY), -1).transpose(1, 0, 2)
        grad_vectors = jnp.sum(lax.all_to_all(vec_blocks, EVERY, 0, 0, tiled=True), axis=0)
    grad_down = down_grads.step().value
    grad_up = up_grads.step().value
    grad_out = out_grads.step().value
    grad_matrices = jnp.concatenate([grad_qkv, grad_out, grad_up, grad_down], axis=1)
    new_matrices, new_first, new_second = adam_update(
        matrices, grad_matrices, first_moment, second_moment, decay_rate
    )
    new_vectors, new_vec_first, new_vec_second = adam_update(
        vectors, grad_vectors, vec_first, vec_second, 0.0
    )
    return (
        outputs[None],
        grad_input[None],
        grad_matrices,
        grad_vectors,
        new_matrices,
        new_vectors,
        new_first,
        new_second,
        new_vec_first,
        new_vec_second,
    )


def solution(mesh):
    ctx, shard = mesh.shape["ctx"], mesh.shape["shard"]
    mesh = Mesh(mesh.devices.reshape(ctx // 2, 2, shard // 2, 2), EVERY)
    placed = (
        P(("x", "c"), CTX, None),
        P(("x", "c"), CTX, None),
        P(("x", "c")),
        P(EVERY, None),
        P(None, EVERY),
        P(EVERY, None),
        P(EVERY, None),
        P(None, EVERY),
        P(None, EVERY),
    )
    return jax.shard_map(
        local,
        mesh=mesh,
        in_specs=placed,
        out_specs=(
            P(("x", "c"), CTX, None),
            P(("x", "c"), CTX, None),
            P(EVERY, None),
            P(None, EVERY),
            P(EVERY, None),
            P(None, EVERY),
            P(EVERY, None),
            P(EVERY, None),
            P(None, EVERY),
            P(None, EVERY),
        ),
        check_vma=False,
    )
```

```python
import functools

import jax
import jax.numpy as jnp
from jax import lax
from jax.experimental import pallas as pl
from jax.experimental.pallas import tpu as pltpu
from jax.sharding import Mesh, PartitionSpec as P


HDIM = 64
STEP = 5


beta_first = 0.9
beta_second = 0.999
learn_rate = 0.02
decay_rate = 0.01
adam_eps = 1e-08
norm_eps = 1e-06


def norm_forward(resid, gain_row, shift_row):
    centered = resid - jnp.mean(resid, axis=-1, keepdims=True)
    inverse = lax.rsqrt(jnp.mean(centered * centered, axis=-1, keepdims=True) + norm_eps)
    normed = centered * inverse
    return (normed * gain_row + shift_row, normed, inverse)


def norm_backward(upstream, gain_row, normed, inverse):
    scaled = upstream * gain_row
    return inverse * (
        scaled
        - jnp.mean(scaled, axis=-1, keepdims=True)
        - normed * jnp.mean(scaled * normed, axis=-1, keepdims=True)
    )


def gelu_parts(preact):
    cumulative = 0.5 * (1.0 + lax.erf(preact * 0.7071067811865476))
    density = jnp.exp(-0.5 * preact * preact) * 0.3989422804014327
    return (preact * cumulative, cumulative + preact * density)


def contract_rows(left, right):
    return lax.dot_general(
        left, right, (((0,), (0,)), ((), ())), preferred_element_type=jnp.float32
    )


def contract_cols(left, right):
    return lax.dot_general(
        left, right, (((1,), (1,)), ((), ())), preferred_element_type=jnp.float32
    )


def adam_update(weights, grads, first, second, decay):
    new_first = beta_first * first + (1.0 - beta_first) * grads
    new_second = beta_second * second + (1.0 - beta_second) * grads * grads
    corr_first = 1.0 - beta_first**STEP
    corr_second = 1.0 - beta_second**STEP
    update = new_first / corr_first / (jnp.sqrt(new_second / corr_second) + adam_eps)
    new_weights = weights.astype(jnp.float32) * (1.0 - learn_rate * decay) - learn_rate * update
    return (new_weights, new_first, new_second)


def column_group(array, col_start, group_width, heads_in):
    return lax.dynamic_slice_in_dim(array, col_start, group_width, 1).reshape(
        array.shape[0], heads_in, HDIM
    )


def group_forward(queries, keys_all, values_all, valid_keys, group_width):
    row_count = queries.shape[0]
    heads_in = group_width // HDIM

    def one_group(group_index):
        col_start = group_index * group_width
        query_g = column_group(queries, col_start, group_width, heads_in)
        key_g = column_group(keys_all, col_start, group_width, heads_in)
        value_g = column_group(values_all, col_start, group_width, heads_in)
        scores = jnp.einsum("qhd,khd->hqk", query_g, key_g, preferred_element_type=jnp.float32)
        logsum = jnp.log(jnp.sum(jnp.where(valid_keys, jnp.exp(scores), 0.0), axis=2))
        attn_probs = jnp.where(valid_keys, jnp.exp(scores - logsum[:, :, None]), 0.0).astype(
            jnp.bfloat16
        )
        group_out = jnp.einsum(
            "hqk,khd->qhd", attn_probs, value_g, preferred_element_type=jnp.float32
        )
        return (group_out.reshape(row_count, group_width).astype(jnp.bfloat16), logsum)

    groups = queries.shape[1] // group_width
    group_outs, logsums = lax.map(one_group, jnp.arange(groups, dtype=jnp.int32))
    return (group_outs.transpose(1, 0, 2).reshape(row_count, groups * group_width), logsums)


def group_backward(
    queries, keys_all, values_all, mixed, grad_mixed, logsums, valid_keys, group_width
):
    row_count = queries.shape[0]
    key_count = keys_all.shape[0]
    heads_in = group_width // HDIM
    head_scale = HDIM ** (-0.5)

    def one_group(items):
        group_index, logsum = items
        col_start = group_index * group_width
        query_g = column_group(queries, col_start, group_width, heads_in)
        key_g = column_group(keys_all, col_start, group_width, heads_in)
        value_g = column_group(values_all, col_start, group_width, heads_in)
        mixed_g = column_group(mixed, col_start, group_width, heads_in)
        grad_g = column_group(grad_mixed, col_start, group_width, heads_in)
        scores = jnp.einsum("qhd,khd->hqk", query_g, key_g, preferred_element_type=jnp.float32)
        probs_full = jnp.where(valid_keys, jnp.exp(scores - logsum[:, :, None]), 0.0)
        probs_low = probs_full.astype(jnp.bfloat16)
        grad_probs = jnp.einsum("qhd,khd->hqk", grad_g, value_g, preferred_element_type=jnp.float32)
        row_delta = jnp.sum(grad_g.astype(jnp.float32) * mixed_g.astype(jnp.float32), axis=2).T
        grad_scores = (probs_full * (grad_probs - row_delta[:, :, None])).astype(jnp.bfloat16)
        grad_query = (
            jnp.einsum("hqk,khd->qhd", grad_scores, key_g, preferred_element_type=jnp.float32)
            * head_scale
        )
        grad_key = jnp.einsum(
            "hqk,qhd->khd", grad_scores, query_g, preferred_element_type=jnp.float32
        )
        grad_value = jnp.einsum(
            "hqk,qhd->khd", probs_low, grad_g, preferred_element_type=jnp.float32
        )
        return (
            grad_query.reshape(row_count, group_width),
            grad_key.reshape(key_count, group_width),
            grad_value.reshape(key_count, group_width),
        )

    groups = queries.shape[1] // group_width
    stacked = lax.map(one_group, (jnp.arange(groups, dtype=jnp.int32), logsums))
    return tuple(
        (
            piece.transpose(1, 0, 2).reshape(piece.shape[1], groups * group_width)
            for piece in stacked
        )
    )


CTX = ("a", "b")
EVERY = ("a", "b", "x", "c")


def shift(array, axis, by=1):
    count = lax.axis_size(axis)
    return lax.ppermute(array, axis, [(i, (i + by) % count) for i in range(count)])


class Line:
    def __init__(self):
        self.last = None

    def tie(self, *arrays):
        if self.last is None:
            return arrays if len(arrays) > 1 else arrays[0]
        tied = lax.optimization_barrier(arrays + self.last)[: len(arrays)]
        return tied if len(arrays) > 1 else tied[0]

    def mark(self, *arrays):
        self.last = arrays
        return arrays if len(arrays) > 1 else arrays[0]


class Chain:
    def __init__(self, line, steps):
        self.line, self.steps, self.value = line, steps, None
        next(steps)

    def step(self):
        try:
            next(self.steps)
        except StopIteration as stop:
            self.value = stop.value
        return self


def pair_gather(line, piece, axis, dim):
    moved = shift(piece, axis)
    yield
    moved = line.tie(moved)
    first = lax.axis_index(axis) == 0
    both = [jnp.where(first, piece, moved), jnp.where(first, moved, piece)]
    return line.mark(jnp.stack(both, axis=dim))


def spread(piece, axes):
    copies = jnp.broadcast_to(piece, (lax.axis_size(axes),) + piece.shape)
    return lax.all_to_all(copies, axes, 0, 0, tiled=True)


def stage_scatter(line, jobs):
    moved, kept = [], []
    for terms, axis, dim, _ in jobs:
        count, index = lax.axis_size(axis), lax.axis_index(axis)
        cut = [
            lax.dynamic_index_in_dim(terms, lax.rem(index + s, count), dim, keepdims=False)
            for s in range(count)
        ]
        moved.append([shift(cut[s], axis, s) for s in range(1, count)])
        kept.append(cut[0])
    yield
    results = []
    for (_, _, _, kind), parts, own in zip(jobs, moved, kept):
        parts = line.tie(*parts) if len(parts) > 1 else [line.tie(parts[0])]
        total = sum((p.astype(jnp.float32) for p in parts), own.astype(jnp.float32))
        results.append(total.astype(kind))
    line.mark(results[-1])
    return results


def line_gather(line, rows):
    count, index = lax.axis_size("a"), lax.axis_index("a")
    moved = [rows] + [shift(rows, "a", step) for step in range(1, count)]
    yield
    lined = jnp.zeros((count,) + rows.shape, rows.dtype)
    for step, part in enumerate(line.tie(*moved)):
        place = lax.rem(index - step + count, count)
        lined = lax.dynamic_update_index_in_dim(lined, part, place, 0)
    return line.mark(lined)


def token_rows(line, rows):
    lined = yield from line_gather(line, rows)
    lined = yield from pair_gather(line, lined, "b", 1)
    return lined.reshape(-1, rows.shape[1])


def all_rows(rows):
    return lax.all_gather(rows, EVERY, axis=0, tiled=True)


def scatter_steps(line, terms, stages):
    for axis, dim, kind in stages:
        (terms,) = yield from stage_scatter(line, [(terms, axis, dim, kind)])
    return terms


def reordered(left):
    width = left.shape[1]
    sizes = [lax.axis_size(axis) for axis in EVERY]
    lines = sizes[0]
    depth = width // (8 * lines)
    a_, b_, x_, c_ = (lax.axis_index(axis) for axis in EVERY)
    column = lax.broadcasted_iota(jnp.int32, (width, 2 * width), 1)
    row = lax.broadcasted_iota(jnp.int32, (width, 2 * width), 0)
    swapped = column >= width
    column = lax.rem(column, width)
    low, block = lax.rem(column, depth), column // depth
    place, block = lax.rem(block, lines), block // lines
    inner, outer, core = lax.rem(block, 2), lax.rem(block // 2, 2), block // 4
    along_x, along_b = jnp.where(swapped, inner, outer), jnp.where(swapped, outer, inner)
    owner = lax.rem(place + a_, lines) * 8 + lax.rem(along_b + b_, 2) * 4 + lax.rem(along_x + x_, 2) * 2
    owner = owner + lax.rem(core + c_, 2)
    return lax.optimization_barrier((row == owner * depth + low).astype(jnp.bfloat16))


def scatter_grads(line, left, right, order):
    width = left.shape[1]
    depth = width // lax.axis_size(EVERY)
    left = jnp.dot(left, order, preferred_element_type=jnp.float32).astype(jnp.bfloat16)
    half = right.shape[1] // 256 * 128
    sides = ((left[:, :width], right[:, :half]), (left[:, width:], right[:, half:]))
    axes = (("c", "x", "b"), ("c", "b", "x"))
    got = [[], []]
    size = width
    for stage in range(3):
        size //= 2
        terms = []
        for side, (rows, columns) in enumerate(sides):
            term = contract_rows(rows[:, size : 2 * size], columns)
            for part in got[side]:
                term = term + part[size : 2 * size].astype(jnp.float32)
            terms.append(term.astype(jnp.bfloat16))
        line.mark(*terms)
        sent = [shift(term, axis[stage]) for term, axis in zip(terms, axes)]
        yield
        sent = line.tie(*sent)
        for side in range(2):
            got[side].append(sent[side])
    lines = []
    for side, (rows, columns) in enumerate(sides):
        term = contract_rows(rows[:, :size], columns)
        for part in got[side]:
            term = term + part[:size].astype(jnp.float32)
        lines.append(term.astype(jnp.bfloat16))
    lines = jnp.concatenate(lines, axis=1).reshape(-1, depth, right.shape[1])
    moved = [shift(lines[step], "a", step) for step in range(1, lines.shape[0])]
    yield
    moved = line.tie(*moved)
    total = sum((part.astype(jnp.float32) for part in moved), lines[0].astype(jnp.float32))
    return line.mark(total)


def moved_to_heads(line, array):
    moved = lax.all_to_all(array, CTX, 0, 0, tiled=True)
    yield
    return line.mark(line.tie(moved))


def heads_weights(line, rows, vectors, groups, wide):
    depth = rows.shape[0]
    cut = rows.reshape(depth, 3, groups, wide).transpose(2, 0, 1, 3)
    cut = cut.reshape(groups, depth, 3 * wide)
    beside = jnp.pad(vectors.T, ((0, 0), (0, -vectors.shape[0] % 128)))
    beside = jnp.broadcast_to(beside, (groups,) + beside.shape)
    moved = line.mark(jnp.concatenate([cut, beside], axis=2))
    moved = yield from moved_to_heads(line, moved)
    moved = yield from pair_gather(line, moved, "x", 1)
    moved = yield from pair_gather(line, moved, "c", 2)
    moved = moved.reshape(-1, moved.shape[-1])
    return moved[:, : 3 * wide], moved[:, 3 * wide : 3 * wide + vectors.shape[0]].T


def heads_grads(line, terms, vectors, before, groups, wide):
    count = vectors.shape[0]
    beside = jnp.pad(vectors.T, ((0, 0), (0, -count % 128))).astype(jnp.bfloat16)
    terms = jnp.concatenate([terms, beside], axis=1)
    sizes = [groups, lax.axis_size("x"), lax.axis_size("c"), -1, terms.shape[1]]
    low = jnp.bfloat16
    terms = yield from scatter_steps(line, terms.reshape(sizes), (("c", 2, low), ("x", 1, low)))
    terms = line.mark(lax.optimization_barrier((terms, before))[0])
    moved = yield from moved_to_heads(line, terms)
    beside = moved[:, :, 3 * wide : 3 * wide + count].astype(jnp.float32)
    moved = moved[:, :, : 3 * wide].reshape(groups, -1, 3, wide).transpose(1, 2, 0, 3)
    moved = moved.reshape(-1, 3 * groups * wide).astype(jnp.float32)
    return moved, jnp.sum(beside, axis=0).T


def attend_kernel(heads, length_ref, query_ref, key_ref, value_ref, mixed_ref, logsum_ref):
    query, key, value = query_ref[...], key_ref[...], value_ref[...]
    lanes = lax.broadcasted_iota(jnp.int32, (1, query.shape[1]), 1) // HDIM
    valid = lax.broadcasted_iota(jnp.int32, (1, key.shape[0]), 1) < length_ref[0]
    mixed = jnp.zeros(query.shape, jnp.float32)
    logsums = jnp.zeros(query.shape, jnp.float32)
    for head in range(heads):
        mine = lanes == head
        scores = contract_cols(jnp.where(mine, query, jnp.zeros_like(query)), key)
        total = jnp.sum(jnp.where(valid, jnp.exp(scores), 0.0), axis=1, keepdims=True)
        logsum = jnp.log(total)
        probs = jnp.where(valid, jnp.exp(scores - logsum), 0.0).astype(jnp.bfloat16)
        out = jnp.dot(probs, value, preferred_element_type=jnp.float32)
        mixed = jnp.where(mine, out, mixed)
        logsums = jnp.where(mine, logsum, logsums)
    mixed_ref[...] = mixed.astype(jnp.bfloat16)
    logsum_ref[...] = logsums


def attend_back_kernel(
    heads,
    length_ref,
    query_ref,
    key_ref,
    value_ref,
    mixed_ref,
    logsum_ref,
    grad_ref,
    out_ref,
    key_acc,
    value_acc,
):
    step = pl.program_id(0)
    rows, wide = query_ref.shape

    @pl.when(step == 0)
    def _():
        key_acc[...] = jnp.zeros_like(key_acc)
        value_acc[...] = jnp.zeros_like(value_acc)

    query, key, value = query_ref[...], key_ref[...], value_ref[...]
    grad, logsums = grad_ref[...], logsum_ref[...]
    lanes = lax.broadcasted_iota(jnp.int32, (1, wide), 1) // HDIM
    valid = lax.broadcasted_iota(jnp.int32, (1, key.shape[0]), 1) < length_ref[0]
    products = grad.astype(jnp.float32) * mixed_ref[...].astype(jnp.float32)
    grad_query = jnp.zeros(query.shape, jnp.float32)
    for head in range(heads):
        mine = lanes == head
        query_h = jnp.where(mine, query, jnp.zeros_like(query))
        grad_h = jnp.where(mine, grad, jnp.zeros_like(grad))
        logsum = logsums[:, head * HDIM : head * HDIM + 1]
        delta = jnp.sum(jnp.where(mine, products, 0.0), axis=1, keepdims=True)
        scores = contract_cols(query_h, key)
        probs = jnp.where(valid, jnp.exp(scores - logsum), 0.0)
        grad_probs = contract_cols(grad_h, value)
        grad_scores = (probs * (grad_probs - delta)).astype(jnp.bfloat16)
        out = jnp.dot(grad_scores, key, preferred_element_type=jnp.float32)
        grad_query = jnp.where(mine, out, grad_query)
        key_acc[...] += contract_rows(grad_scores, query_h)
        value_acc[...] += contract_rows(probs.astype(jnp.bfloat16), grad_h)
    start = pl.multiple_of(step * rows, rows)
    out_ref[pl.ds(start, rows), :wide] = (grad_query * HDIM ** (-0.5)).astype(jnp.bfloat16)

    @pl.when(step == pl.num_programs(0) - 1)
    def _():
        out_ref[:, wide : 2 * wide] = key_acc[...].astype(jnp.bfloat16)
        out_ref[:, 2 * wide :] = value_acc[...].astype(jnp.bfloat16)


def attend(packed, lengths):
    positions, wide = packed.shape[0], packed.shape[1] // 3
    block = min(256, positions)
    part = lambda which: pl.BlockSpec((positions, wide), lambda i, n: (0, which))
    rows = pl.BlockSpec((block, wide), lambda i, n: (i, 0))
    return pl.pallas_call(
        functools.partial(attend_kernel, wide // HDIM),
        grid_spec=pltpu.PrefetchScalarGridSpec(
            num_scalar_prefetch=1,
            grid=(positions // block,),
            in_specs=[rows, part(1), part(2)],
            out_specs=[rows, rows],
        ),
        out_shape=[
            jax.ShapeDtypeStruct((positions, wide), jnp.bfloat16),
            jax.ShapeDtypeStruct((positions, wide), jnp.float32),
        ],
        cost_estimate=pl.CostEstimate(
            flops=4 * positions * positions * wide,
            transcendentals=2 * positions * positions * wide // HDIM,
            bytes_accessed=12 * positions * wide,
        ),
    )(lengths, packed, packed, packed)


def attend_back(packed, lengths, mixed, logsums, grads):
    positions, wide = mixed.shape
    block = min(256, positions)
    part = lambda which: pl.BlockSpec((positions, wide), lambda i, n: (0, which))
    rows = pl.BlockSpec((block, wide), lambda i, n: (i, 0))
    return pl.pallas_call(
        functools.partial(attend_back_kernel, wide // HDIM),
        grid_spec=pltpu.PrefetchScalarGridSpec(
            num_scalar_prefetch=1,
            grid=(positions // block,),
            in_specs=[rows, part(1), part(2), rows, rows, rows],
            out_specs=pl.BlockSpec((positions, 3 * wide), lambda i, n: (0, 0)),
            scratch_shapes=[pltpu.VMEM((positions, wide), jnp.float32)] * 2,
        ),
        out_shape=jax.ShapeDtypeStruct((positions, 3 * wide), jnp.bfloat16),
        cost_estimate=pl.CostEstimate(
            flops=10 * positions * positions * wide,
            transcendentals=positions * positions * wide // HDIM,
            bytes_accessed=20 * positions * wide,
        ),
    )(lengths, packed, packed, packed, mixed, logsums, grads)


def to_heads(rows, kinds):
    groups = lax.axis_size(CTX)
    count, width = rows.shape
    wide = width // (kinds * groups)
    cut = rows.reshape(count, kinds, groups, wide).transpose(2, 0, 1, 3)
    cut = cut.reshape(groups, count, kinds * wide)
    moved = lax.all_to_all(cut, CTX, 0, 0, tiled=True)
    return moved.reshape(groups * count, kinds * wide)


def to_positions(rows, kinds):
    groups = lax.axis_size(CTX)
    count, wide = rows.shape[0] // groups, rows.shape[1] // kinds
    moved = lax.all_to_all(rows.reshape(groups, count, kinds * wide), CTX, 0, 0, tiled=True)
    moved = moved.reshape(groups, count, kinds, wide).transpose(1, 2, 0, 3)
    return moved.reshape(count, kinds * groups * wide)


def local(
    tokens,
    cotangent,
    lengths,
    matrices,
    vectors,
    first_moment,
    second_moment,
    vec_first,
    vec_second,
):
    inputs = tokens[0]
    upstream = cotangent[0]
    length = lengths[0]
    width = inputs.shape[1]
    group_width = min(width, 256)
    head_scale = HDIM ** (-0.5)
    hidden_width = (matrices.shape[1] - 4 * width) // 2
    vector_count = vectors.shape[0]
    groups = lax.axis_size(CTX)
    wide = width // groups
    by_heads = width % (groups * 128) == 0
    rows_qkv = matrices[:, : 3 * width]
    line = Line()
    chain = lambda make, *args: Chain(line, make(line, *args))
    full_rest = all_rows(matrices[:, 3 * width :])
    weight_out = full_rest[:, :width]
    weight_up = full_rest[:, width : width + hidden_width]
    weight_down = full_rest[:, width + hidden_width :]
    if by_heads:
        heads_chain = chain(heads_weights, rows_qkv, vectors, groups, wide)
        inputs = line.tie(inputs)
        left_chain = chain(token_rows, inputs[:, : width // 2])
        right_chain = chain(token_rows, inputs[:, width // 2 :])
        heads_chain.step()
        left_chain.step()
        heads_chain.step()
        right_chain.step()
        tokens_left = left_chain.step().value
        weight_heads, vector_rows = heads_chain.step().value
        vector_rows = vector_rows.astype(jnp.float32)
        tokens_right = right_chain.step().value
        projected = jnp.dot(
            tokens_left, weight_heads[: width // 2], preferred_element_type=jnp.float32
        ) + jnp.dot(tokens_right, weight_heads[width // 2 :], preferred_element_type=jnp.float32)
        own = lax.dynamic_slice_in_dim(vector_rows, lax.axis_index(CTX) * wide, wide, 1)
        packed = jnp.concatenate(
            [
                (projected[:, :wide] + own[0]) * head_scale,
                projected[:, wide : 2 * wide],
                projected[:, 2 * wide :] + own[1],
            ],
            axis=1,
        ).astype(jnp.bfloat16)
        mixed_heads, logsums = attend(packed, lengths)
        line.mark(mixed_heads)
        mixed = to_positions(mixed_heads, 1)
    else:
        vector_rows = spread(vectors.T, EVERY).reshape(width, vector_count).T.astype(jnp.float32)
        weight_qkv = all_rows(rows_qkv)
        projected = jnp.dot(inputs, weight_qkv, preferred_element_type=jnp.float32)
        queries = ((projected[:, :width] + vector_rows[0]) * head_scale).astype(jnp.bfloat16)
        keys_own = projected[:, width : 2 * width].astype(jnp.bfloat16)
        values_own = (projected[:, 2 * width :] + vector_rows[1]).astype(jnp.bfloat16)
        keys_all, values_all = (
            lax.all_gather(keys_own, CTX, axis=0, tiled=True),
            lax.all_gather(values_own, CTX, axis=0, tiled=True),
        )
        valid_keys = jnp.arange(keys_all.shape[0], dtype=jnp.int32) < length
        mixed, logsums = group_forward(queries, keys_all, values_all, valid_keys, group_width)
    bias_up = vector_rows[8:].reshape(-1)
    resid_one = (
        inputs.astype(jnp.float32)
        + jnp.dot(mixed, weight_out, preferred_element_type=jnp.float32)
        + vector_rows[2]
    )
    hidden, normed_one, inverse_one = norm_forward(resid_one, vector_rows[3], vector_rows[4])
    hidden_low = hidden.astype(jnp.bfloat16)
    preact = jnp.dot(hidden_low, weight_up, preferred_element_type=jnp.float32) + bias_up
    activ_full, gelu_slope = gelu_parts(preact)
    activated = activ_full.astype(jnp.bfloat16)
    resid_two = hidden + contract_cols(activated, weight_down) + vector_rows[5]
    outputs, normed_two, inverse_two = norm_forward(resid_two, vector_rows[6], vector_rows[7])
    grad_resid_two = norm_backward(upstream, vector_rows[6], normed_two, inverse_two)
    grad_two_low = grad_resid_two.astype(jnp.bfloat16)
    if by_heads:
        weight_qkv = all_rows(lax.optimization_barrier((rows_qkv, packed))[0])
    order = reordered(inputs)
    line.mark(grad_two_low)
    down_grads = chain(scatter_grads, grad_two_low, activated, order)
    grad_preact = jnp.dot(line.tie(grad_two_low), weight_down, preferred_element_type=jnp.float32)
    grad_preact = grad_preact * gelu_slope
    grad_preact_low = line.mark(grad_preact.astype(jnp.bfloat16))
    up_grads = chain(scatter_grads, hidden_low, grad_preact_low, order)
    down_grads.step()
    grad_hidden = grad_resid_two + contract_cols(line.tie(grad_preact_low), weight_up)
    grad_resid_one = norm_backward(grad_hidden, vector_rows[3], normed_one, inverse_one)
    grad_one_low = grad_resid_one.astype(jnp.bfloat16)
    grad_mixed = contract_cols(grad_one_low, weight_out).astype(jnp.bfloat16)
    line.mark(grad_mixed)
    def vector_terms(query_sum, value_sum):
        small_rows = jnp.stack(
            [
                query_sum,
                value_sum,
                jnp.sum(grad_resid_one, axis=0),
                jnp.sum(grad_hidden * normed_one, axis=0),
                jnp.sum(grad_hidden, axis=0),
                jnp.sum(grad_resid_two, axis=0),
                jnp.sum(upstream * normed_two, axis=0),
                jnp.sum(upstream, axis=0),
            ]
        )
        return jnp.concatenate(
            [small_rows, jnp.sum(grad_preact, axis=0).reshape(-1, width)], axis=0
        )

    if by_heads:
        grad_all = to_heads(grad_mixed, 1)
        out_grads = chain(scatter_grads, mixed, grad_one_low, order)
        up_grads.step()
        down_grads.step()
        out_grads.step()
        grad_heads = attend_back(packed, lengths, mixed_heads, logsums, line.tie(grad_all))
        line.mark(grad_heads)
        grad_proj = to_positions(grad_heads, 3)
        sums = jnp.sum(grad_heads.astype(jnp.float32), axis=0).reshape(3, wide)
        all_sums = jnp.zeros((3, groups, wide), jnp.float32)
        all_sums = lax.dynamic_update_index_in_dim(all_sums, sums, lax.axis_index(CTX), 1)
        all_sums = all_sums.reshape(3, width)
        query_sum, value_sum = all_sums[0], all_sums[2]
        grad_cols = jnp.concatenate(
            [contract_rows(tokens_left, grad_heads), contract_rows(tokens_right, grad_heads)]
        ).astype(jnp.bfloat16)
        heads_chain = chain(
            heads_grads, grad_cols, vector_terms(query_sum, value_sum), grad_proj, groups, wide
        )
        up_grads.step()
        heads_chain.step()
        down_grads.step()
        out_grads.step()
        heads_chain.step()
        up_grads.step()
        out_grads.step()
    else:
        up_grads.step()
        out_grads = chain(scatter_grads, mixed, grad_one_low, order)
        for made in (down_grads, up_grads) * 2 + (out_grads,) * 3:
            made.step()
        grad_query, key_terms, value_terms = group_backward(
            queries, keys_all, values_all, mixed, grad_mixed, logsums, valid_keys, group_width
        )
        grad_key, grad_value = (
            lax.psum_scatter(
                terms.astype(jnp.bfloat16), CTX, scatter_dimension=0, tiled=True
            ).astype(jnp.float32)
            for terms in (key_terms, value_terms)
        )
        grad_proj = jnp.concatenate([grad_query, grad_key, grad_value], axis=1).astype(jnp.bfloat16)
        query_sum, value_sum = jnp.sum(grad_query, axis=0), jnp.sum(grad_value, axis=0)
        qkv_grads = chain(scatter_grads, inputs, grad_proj, order)
        for _ in range(3):
            qkv_grads.step()
    grad_input = grad_resid_one + contract_cols(grad_proj, weight_qkv)
    if by_heads:
        grad_qkv, grad_vectors = heads_chain.step().value
    else:
        grad_qkv = qkv_grads.step().value
        vec_blocks = vector_terms(query_sum, value_sum)
        vec_blocks = vec_blocks.reshape(vector_count, lax.axis_size(EVERY), -1).transpose(1, 0, 2)
        grad_vectors = jnp.sum(lax.all_to_all(vec_blocks, EVERY, 0, 0, tiled=True), axis=0)
    grad_down = down_grads.step().value
    grad_up = up_grads.step().value
    grad_out = out_grads.step().value
    grad_matrices = jnp.concatenate([grad_qkv, grad_out, grad_up, grad_down], axis=1)
    new_matrices, new_first, new_second = adam_update(
        matrices, grad_matrices, first_moment, second_moment, decay_rate
    )
    new_vectors, new_vec_first, new_vec_second = adam_update(
        vectors, grad_vectors, vec_first, vec_second, 0.0
    )
    return (
        outputs[None],
        grad_input[None],
        grad_matrices,
        grad_vectors,
        new_matrices,
        new_vectors,
        new_first,
        new_second,
        new_vec_first,
        new_vec_second,
    )


def solution(mesh):
    ctx, shard = mesh.shape["ctx"], mesh.shape["shard"]
    mesh = Mesh(mesh.devices.reshape(ctx // 2, 2, shard // 2, 2), EVERY)
    placed = (
        P(("x", "c"), CTX, None),
        P(("x", "c"), CTX, None),
        P(("x", "c")),
        P(EVERY, None),
        P(None, EVERY),
        P(EVERY, None),
        P(EVERY, None),
        P(None, EVERY),
        P(None, EVERY),
    )
    return jax.shard_map(
        local,
        mesh=mesh,
        in_specs=placed,
        out_specs=(
            P(("x", "c"), CTX, None),
            P(("x", "c"), CTX, None),
            P(EVERY, None),
            P(None, EVERY),
            P(EVERY, None),
            P(None, EVERY),
            P(EVERY, None),
            P(EVERY, None),
            P(None, EVERY),
            P(None, EVERY),
        ),
        check_vma=False,
    )
```

```python
import functools

import jax
import jax.numpy as jnp
from jax import lax
from jax.experimental import pallas as pl
from jax.experimental.pallas import tpu as pltpu
from jax.sharding import Mesh, PartitionSpec as P


HDIM = 64
STEP = 5


beta_first = 0.9
beta_second = 0.999
learn_rate = 0.02
decay_rate = 0.01
adam_eps = 1e-08
norm_eps = 1e-06


def norm_forward(resid, gain_row, shift_row):
    centered = resid - jnp.mean(resid, axis=-1, keepdims=True)
    inverse = lax.rsqrt(jnp.mean(centered * centered, axis=-1, keepdims=True) + norm_eps)
    normed = centered * inverse
    return (normed * gain_row + shift_row, normed, inverse)


def norm_backward(upstream, gain_row, normed, inverse):
    scaled = upstream * gain_row
    return inverse * (
        scaled
        - jnp.mean(scaled, axis=-1, keepdims=True)
        - normed * jnp.mean(scaled * normed, axis=-1, keepdims=True)
    )


def gelu_parts(preact):
    cumulative = 0.5 * (1.0 + lax.erf(preact * 0.7071067811865476))
    density = jnp.exp(-0.5 * preact * preact) * 0.3989422804014327
    return (preact * cumulative, cumulative + preact * density)


def contract_rows(left, right):
    return lax.dot_general(
        left, right, (((0,), (0,)), ((), ())), preferred_element_type=jnp.float32
    )


def contract_cols(left, right):
    return lax.dot_general(
        left, right, (((1,), (1,)), ((), ())), preferred_element_type=jnp.float32
    )


def adam_update(weights, grads, first, second, decay):
    new_first = beta_first * first + (1.0 - beta_first) * grads
    new_second = beta_second * second + (1.0 - beta_second) * grads * grads
    corr_first = 1.0 - beta_first**STEP
    corr_second = 1.0 - beta_second**STEP
    update = new_first / corr_first / (jnp.sqrt(new_second / corr_second) + adam_eps)
    new_weights = weights.astype(jnp.float32) * (1.0 - learn_rate * decay) - learn_rate * update
    return (new_weights, new_first, new_second)


def column_group(array, col_start, group_width, heads_in):
    return lax.dynamic_slice_in_dim(array, col_start, group_width, 1).reshape(
        array.shape[0], heads_in, HDIM
    )


def group_forward(queries, keys_all, values_all, valid_keys, group_width):
    row_count = queries.shape[0]
    heads_in = group_width // HDIM

    def one_group(group_index):
        col_start = group_index * group_width
        query_g = column_group(queries, col_start, group_width, heads_in)
        key_g = column_group(keys_all, col_start, group_width, heads_in)
        value_g = column_group(values_all, col_start, group_width, heads_in)
        scores = jnp.einsum("qhd,khd->hqk", query_g, key_g, preferred_element_type=jnp.float32)
        logsum = jnp.log(jnp.sum(jnp.where(valid_keys, jnp.exp(scores), 0.0), axis=2))
        attn_probs = jnp.where(valid_keys, jnp.exp(scores - logsum[:, :, None]), 0.0).astype(
            jnp.bfloat16
        )
        group_out = jnp.einsum(
            "hqk,khd->qhd", attn_probs, value_g, preferred_element_type=jnp.float32
        )
        return (group_out.reshape(row_count, group_width).astype(jnp.bfloat16), logsum)

    groups = queries.shape[1] // group_width
    group_outs, logsums = lax.map(one_group, jnp.arange(groups, dtype=jnp.int32))
    return (group_outs.transpose(1, 0, 2).reshape(row_count, groups * group_width), logsums)


def group_backward(
    queries, keys_all, values_all, mixed, grad_mixed, logsums, valid_keys, group_width
):
    row_count = queries.shape[0]
    key_count = keys_all.shape[0]
    heads_in = group_width // HDIM
    head_scale = HDIM ** (-0.5)

    def one_group(items):
        group_index, logsum = items
        col_start = group_index * group_width
        query_g = column_group(queries, col_start, group_width, heads_in)
        key_g = column_group(keys_all, col_start, group_width, heads_in)
        value_g = column_group(values_all, col_start, group_width, heads_in)
        mixed_g = column_group(mixed, col_start, group_width, heads_in)
        grad_g = column_group(grad_mixed, col_start, group_width, heads_in)
        scores = jnp.einsum("qhd,khd->hqk", query_g, key_g, preferred_element_type=jnp.float32)
        probs_full = jnp.where(valid_keys, jnp.exp(scores - logsum[:, :, None]), 0.0)
        probs_low = probs_full.astype(jnp.bfloat16)
        grad_probs = jnp.einsum("qhd,khd->hqk", grad_g, value_g, preferred_element_type=jnp.float32)
        row_delta = jnp.sum(grad_g.astype(jnp.float32) * mixed_g.astype(jnp.float32), axis=2).T
        grad_scores = (probs_full * (grad_probs - row_delta[:, :, None])).astype(jnp.bfloat16)
        grad_query = (
            jnp.einsum("hqk,khd->qhd", grad_scores, key_g, preferred_element_type=jnp.float32)
            * head_scale
        )
        grad_key = jnp.einsum(
            "hqk,qhd->khd", grad_scores, query_g, preferred_element_type=jnp.float32
        )
        grad_value = jnp.einsum(
            "hqk,qhd->khd", probs_low, grad_g, preferred_element_type=jnp.float32
        )
        return (
            grad_query.reshape(row_count, group_width),
            grad_key.reshape(key_count, group_width),
            grad_value.reshape(key_count, group_width),
        )

    groups = queries.shape[1] // group_width
    stacked = lax.map(one_group, (jnp.arange(groups, dtype=jnp.int32), logsums))
    return tuple(
        (
            piece.transpose(1, 0, 2).reshape(piece.shape[1], groups * group_width)
            for piece in stacked
        )
    )


CTX = ("a", "b")
EVERY = ("a", "b", "x", "c")


def shift(array, axis, by=1):
    count = lax.axis_size(axis)
    return lax.ppermute(array, axis, [(i, (i + by) % count) for i in range(count)])


class Line:
    def __init__(self):
        self.last = None

    def tie(self, *arrays):
        if self.last is None:
            return arrays if len(arrays) > 1 else arrays[0]
        tied = lax.optimization_barrier(arrays + self.last)[: len(arrays)]
        return tied if len(arrays) > 1 else tied[0]

    def mark(self, *arrays):
        self.last = arrays
        return arrays if len(arrays) > 1 else arrays[0]


class Chain:
    def __init__(self, line, steps):
        self.line, self.steps, self.value = line, steps, None
        next(steps)

    def step(self):
        try:
            next(self.steps)
        except StopIteration as stop:
            self.value = stop.value
        return self


def pair_gather(line, piece, axis, dim):
    moved = shift(piece, axis)
    yield
    moved = line.tie(moved)
    first = lax.axis_index(axis) == 0
    both = [jnp.where(first, piece, moved), jnp.where(first, moved, piece)]
    return line.mark(jnp.stack(both, axis=dim))


def spread(piece, axes):
    copies = jnp.broadcast_to(piece, (lax.axis_size(axes),) + piece.shape)
    return lax.all_to_all(copies, axes, 0, 0, tiled=True)


def stage_scatter(line, jobs):
    moved, kept = [], []
    for terms, axis, dim, _ in jobs:
        count, index = lax.axis_size(axis), lax.axis_index(axis)
        cut = [
            lax.dynamic_index_in_dim(terms, lax.rem(index + s, count), dim, keepdims=False)
            for s in range(count)
        ]
        moved.append([shift(cut[s], axis, s) for s in range(1, count)])
        kept.append(cut[0])
    yield
    results = []
    for (_, _, _, kind), parts, own in zip(jobs, moved, kept):
        parts = line.tie(*parts) if len(parts) > 1 else [line.tie(parts[0])]
        total = sum((p.astype(jnp.float32) for p in parts), own.astype(jnp.float32))
        results.append(total.astype(kind))
    line.mark(results[-1])
    return results


def line_gather(line, rows):
    count, index = lax.axis_size("a"), lax.axis_index("a")
    moved = [rows] + [shift(rows, "a", step) for step in range(1, count)]
    yield
    lined = jnp.zeros((count,) + rows.shape, rows.dtype)
    for step, part in enumerate(line.tie(*moved)):
        place = lax.rem(index - step + count, count)
        lined = lax.dynamic_update_index_in_dim(lined, part, place, 0)
    return line.mark(lined)


def token_rows(line, rows):
    lined = yield from line_gather(line, rows)
    lined = yield from pair_gather(line, lined, "b", 1)
    return lined.reshape(-1, rows.shape[1])


def all_rows(rows):
    return lax.all_gather(rows, EVERY, axis=0, tiled=True)


def scatter_steps(line, terms, stages):
    for axis, dim, kind in stages:
        (terms,) = yield from stage_scatter(line, [(terms, axis, dim, kind)])
    return terms


def reordered(left):
    width = left.shape[1]
    sizes = [lax.axis_size(axis) for axis in EVERY]
    lines = sizes[0]
    depth = width // (8 * lines)
    a_, b_, x_, c_ = (lax.axis_index(axis) for axis in EVERY)
    column = lax.broadcasted_iota(jnp.int32, (width, 2 * width), 1)
    row = lax.broadcasted_iota(jnp.int32, (width, 2 * width), 0)
    swapped = column >= width
    column = lax.rem(column, width)
    low, block = lax.rem(column, depth), column // depth
    place, block = lax.rem(block, lines), block // lines
    inner, outer, core = lax.rem(block, 2), lax.rem(block // 2, 2), block // 4
    along_x, along_b = jnp.where(swapped, inner, outer), jnp.where(swapped, outer, inner)
    owner = lax.rem(place + a_, lines) * 8 + lax.rem(along_b + b_, 2) * 4 + lax.rem(along_x + x_, 2) * 2
    owner = owner + lax.rem(core + c_, 2)
    return lax.optimization_barrier((row == owner * depth + low).astype(jnp.bfloat16))


def scatter_grads(line, left, right, order):
    width = left.shape[1]
    depth = width // lax.axis_size(EVERY)
    left = jnp.dot(left, order, preferred_element_type=jnp.float32).astype(jnp.bfloat16)
    half = right.shape[1] // 256 * 128
    sides = ((left[:, :width], right[:, :half]), (left[:, width:], right[:, half:]))
    axes = (("c", "x", "b"), ("c", "b", "x"))
    got = [[], []]
    size = width
    for stage in range(3):
        size //= 2
        terms = []
        for side, (rows, columns) in enumerate(sides):
            term = contract_rows(rows[:, size : 2 * size], columns)
            for part in got[side]:
                term = term + part[size : 2 * size].astype(jnp.float32)
            terms.append(term.astype(jnp.bfloat16))
        line.mark(*terms)
        sent = [shift(term, axis[stage]) for term, axis in zip(terms, axes)]
        yield
        *sent, left = line.tie(*sent, left)
        sides = ((left[:, :width], right[:, :half]), (left[:, width:], right[:, half:]))
        for side in range(2):
            got[side].append(sent[side])
    lines = []
    for side, (rows, columns) in enumerate(sides):
        term = contract_rows(rows[:, :size], columns)
        for part in got[side]:
            term = term + part[:size].astype(jnp.float32)
        lines.append(term.astype(jnp.bfloat16))
    lines = jnp.concatenate(lines, axis=1).reshape(-1, depth, right.shape[1])
    moved = [shift(lines[step], "a", step) for step in range(1, lines.shape[0])]
    yield
    moved = line.tie(*moved)
    total = sum((part.astype(jnp.float32) for part in moved), lines[0].astype(jnp.float32))
    return line.mark(total)


def moved_to_heads(line, array):
    moved = lax.all_to_all(array, CTX, 0, 0, tiled=True)
    yield
    return line.mark(line.tie(moved))


def heads_weights(line, rows, vectors, groups, wide):
    depth = rows.shape[0]
    cut = rows.reshape(depth, 3, groups, wide).transpose(2, 0, 1, 3)
    cut = cut.reshape(groups, depth, 3 * wide)
    beside = jnp.pad(vectors.T, ((0, 0), (0, -vectors.shape[0] % 128)))
    beside = jnp.broadcast_to(beside, (groups,) + beside.shape)
    moved = line.mark(jnp.concatenate([cut, beside], axis=2))
    moved = yield from moved_to_heads(line, moved)
    moved = yield from pair_gather(line, moved, "x", 1)
    moved = yield from pair_gather(line, moved, "c", 2)
    moved = moved.reshape(-1, moved.shape[-1])
    return moved[:, : 3 * wide], moved[:, 3 * wide : 3 * wide + vectors.shape[0]].T


def heads_grads(line, terms, vectors, before, groups, wide):
    count = vectors.shape[0]
    beside = jnp.pad(vectors.T, ((0, 0), (0, -count % 128))).astype(jnp.bfloat16)
    terms = jnp.concatenate([terms, beside], axis=1)
    sizes = [groups, lax.axis_size("x"), lax.axis_size("c"), -1, terms.shape[1]]
    low = jnp.bfloat16
    terms = yield from scatter_steps(line, terms.reshape(sizes), (("c", 2, low), ("x", 1, low)))
    terms = line.mark(lax.optimization_barrier((terms, before))[0])
    moved = yield from moved_to_heads(line, terms)
    beside = moved[:, :, 3 * wide : 3 * wide + count].astype(jnp.float32)
    moved = moved[:, :, : 3 * wide].reshape(groups, -1, 3, wide).transpose(1, 2, 0, 3)
    moved = moved.reshape(-1, 3 * groups * wide).astype(jnp.float32)
    return moved, jnp.sum(beside, axis=0).T


def attend_kernel(heads, length_ref, query_ref, key_ref, value_ref, mixed_ref, logsum_ref):
    query, key, value = query_ref[...], key_ref[...], value_ref[...]
    lanes = lax.broadcasted_iota(jnp.int32, (1, query.shape[1]), 1) // HDIM
    valid = lax.broadcasted_iota(jnp.int32, (1, key.shape[0]), 1) < length_ref[0]
    mixed = jnp.zeros(query.shape, jnp.float32)
    logsums = jnp.zeros(query.shape, jnp.float32)
    for head in range(heads):
        mine = lanes == head
        scores = contract_cols(jnp.where(mine, query, jnp.zeros_like(query)), key)
        total = jnp.sum(jnp.where(valid, jnp.exp(scores), 0.0), axis=1, keepdims=True)
        logsum = jnp.log(total)
        probs = jnp.where(valid, jnp.exp(scores - logsum), 0.0).astype(jnp.bfloat16)
        out = jnp.dot(probs, value, preferred_element_type=jnp.float32)
        mixed = jnp.where(mine, out, mixed)
        logsums = jnp.where(mine, logsum, logsums)
    mixed_ref[...] = mixed.astype(jnp.bfloat16)
    logsum_ref[...] = logsums


def attend_back_kernel(
    heads,
    length_ref,
    query_ref,
    key_ref,
    value_ref,
    mixed_ref,
    logsum_ref,
    grad_ref,
    out_ref,
    key_acc,
    value_acc,
):
    step = pl.program_id(0)
    rows, wide = query_ref.shape

    @pl.when(step == 0)
    def _():
        key_acc[...] = jnp.zeros_like(key_acc)
        value_acc[...] = jnp.zeros_like(value_acc)

    query, key, value = query_ref[...], key_ref[...], value_ref[...]
    grad, logsums = grad_ref[...], logsum_ref[...]
    lanes = lax.broadcasted_iota(jnp.int32, (1, wide), 1) // HDIM
    valid = lax.broadcasted_iota(jnp.int32, (1, key.shape[0]), 1) < length_ref[0]
    products = grad.astype(jnp.float32) * mixed_ref[...].astype(jnp.float32)
    grad_query = jnp.zeros(query.shape, jnp.float32)
    for head in range(heads):
        mine = lanes == head
        query_h = jnp.where(mine, query, jnp.zeros_like(query))
        grad_h = jnp.where(mine, grad, jnp.zeros_like(grad))
        logsum = logsums[:, head * HDIM : head * HDIM + 1]
        delta = jnp.sum(jnp.where(mine, products, 0.0), axis=1, keepdims=True)
        scores = contract_cols(query_h, key)
        probs = jnp.where(valid, jnp.exp(scores - logsum), 0.0)
        grad_probs = contract_cols(grad_h, value)
        grad_scores = (probs * (grad_probs - delta)).astype(jnp.bfloat16)
        out = jnp.dot(grad_scores, key, preferred_element_type=jnp.float32)
        grad_query = jnp.where(mine, out, grad_query)
        key_acc[...] += contract_rows(grad_scores, query_h)
        value_acc[...] += contract_rows(probs.astype(jnp.bfloat16), grad_h)
    start = pl.multiple_of(step * rows, rows)
    out_ref[pl.ds(start, rows), :wide] = (grad_query * HDIM ** (-0.5)).astype(jnp.bfloat16)

    @pl.when(step == pl.num_programs(0) - 1)
    def _():
        out_ref[:, wide : 2 * wide] = key_acc[...].astype(jnp.bfloat16)
        out_ref[:, 2 * wide :] = value_acc[...].astype(jnp.bfloat16)


def attend(packed, lengths):
    positions, wide = packed.shape[0], packed.shape[1] // 3
    block = min(256, positions)
    part = lambda which: pl.BlockSpec((positions, wide), lambda i, n: (0, which))
    rows = pl.BlockSpec((block, wide), lambda i, n: (i, 0))
    return pl.pallas_call(
        functools.partial(attend_kernel, wide // HDIM),
        grid_spec=pltpu.PrefetchScalarGridSpec(
            num_scalar_prefetch=1,
            grid=(positions // block,),
            in_specs=[rows, part(1), part(2)],
            out_specs=[rows, rows],
        ),
        out_shape=[
            jax.ShapeDtypeStruct((positions, wide), jnp.bfloat16),
            jax.ShapeDtypeStruct((positions, wide), jnp.float32),
        ],
        cost_estimate=pl.CostEstimate(
            flops=4 * positions * positions * wide,
            transcendentals=2 * positions * positions * wide // HDIM,
            bytes_accessed=12 * positions * wide,
        ),
    )(lengths, packed, packed, packed)


def attend_back(packed, lengths, mixed, logsums, grads):
    positions, wide = mixed.shape
    block = min(256, positions)
    part = lambda which: pl.BlockSpec((positions, wide), lambda i, n: (0, which))
    rows = pl.BlockSpec((block, wide), lambda i, n: (i, 0))
    return pl.pallas_call(
        functools.partial(attend_back_kernel, wide // HDIM),
        grid_spec=pltpu.PrefetchScalarGridSpec(
            num_scalar_prefetch=1,
            grid=(positions // block,),
            in_specs=[rows, part(1), part(2), rows, rows, rows],
            out_specs=pl.BlockSpec((positions, 3 * wide), lambda i, n: (0, 0)),
            scratch_shapes=[pltpu.VMEM((positions, wide), jnp.float32)] * 2,
        ),
        out_shape=jax.ShapeDtypeStruct((positions, 3 * wide), jnp.bfloat16),
        cost_estimate=pl.CostEstimate(
            flops=10 * positions * positions * wide,
            transcendentals=positions * positions * wide // HDIM,
            bytes_accessed=20 * positions * wide,
        ),
    )(lengths, packed, packed, packed, mixed, logsums, grads)


def to_heads(rows, kinds):
    groups = lax.axis_size(CTX)
    count, width = rows.shape
    wide = width // (kinds * groups)
    cut = rows.reshape(count, kinds, groups, wide).transpose(2, 0, 1, 3)
    cut = cut.reshape(groups, count, kinds * wide)
    moved = lax.all_to_all(cut, CTX, 0, 0, tiled=True)
    return moved.reshape(groups * count, kinds * wide)


def to_positions(rows, kinds):
    groups = lax.axis_size(CTX)
    count, wide = rows.shape[0] // groups, rows.shape[1] // kinds
    moved = lax.all_to_all(rows.reshape(groups, count, kinds * wide), CTX, 0, 0, tiled=True)
    moved = moved.reshape(groups, count, kinds, wide).transpose(1, 2, 0, 3)
    return moved.reshape(count, kinds * groups * wide)


def local(
    tokens,
    cotangent,
    lengths,
    matrices,
    vectors,
    first_moment,
    second_moment,
    vec_first,
    vec_second,
):
    inputs = tokens[0]
    upstream = cotangent[0]
    length = lengths[0]
    width = inputs.shape[1]
    group_width = min(width, 256)
    head_scale = HDIM ** (-0.5)
    hidden_width = (matrices.shape[1] - 4 * width) // 2
    vector_count = vectors.shape[0]
    groups = lax.axis_size(CTX)
    wide = width // groups
    by_heads = width % (groups * 128) == 0
    rows_qkv = matrices[:, : 3 * width]
    line = Line()
    chain = lambda make, *args: Chain(line, make(line, *args))
    full_rest = all_rows(matrices[:, 3 * width :])
    weight_out = full_rest[:, :width]
    weight_up = full_rest[:, width : width + hidden_width]
    weight_down = full_rest[:, width + hidden_width :]
    if by_heads:
        heads_chain = chain(heads_weights, rows_qkv, vectors, groups, wide)
        inputs = line.tie(inputs)
        left_chain = chain(token_rows, inputs[:, : width // 2])
        right_chain = chain(token_rows, inputs[:, width // 2 :])
        heads_chain.step()
        left_chain.step()
        heads_chain.step()
        right_chain.step()
        tokens_left = left_chain.step().value
        weight_heads, vector_rows = heads_chain.step().value
        vector_rows = vector_rows.astype(jnp.float32)
        tokens_right = right_chain.step().value
        projected = jnp.dot(
            tokens_left, weight_heads[: width // 2], preferred_element_type=jnp.float32
        ) + jnp.dot(tokens_right, weight_heads[width // 2 :], preferred_element_type=jnp.float32)
        own = lax.dynamic_slice_in_dim(vector_rows, lax.axis_index(CTX) * wide, wide, 1)
        packed = jnp.concatenate(
            [
                (projected[:, :wide] + own[0]) * head_scale,
                projected[:, wide : 2 * wide],
                projected[:, 2 * wide :] + own[1],
            ],
            axis=1,
        ).astype(jnp.bfloat16)
        mixed_heads, logsums = attend(packed, lengths)
        line.mark(mixed_heads)
        mixed = to_positions(mixed_heads, 1)
    else:
        vector_rows = spread(vectors.T, EVERY).reshape(width, vector_count).T.astype(jnp.float32)
        weight_qkv = all_rows(rows_qkv)
        projected = jnp.dot(inputs, weight_qkv, preferred_element_type=jnp.float32)
        queries = ((projected[:, :width] + vector_rows[0]) * head_scale).astype(jnp.bfloat16)
        keys_own = projected[:, width : 2 * width].astype(jnp.bfloat16)
        values_own = (projected[:, 2 * width :] + vector_rows[1]).astype(jnp.bfloat16)
        keys_all, values_all = (
            lax.all_gather(keys_own, CTX, axis=0, tiled=True),
            lax.all_gather(values_own, CTX, axis=0, tiled=True),
        )
        valid_keys = jnp.arange(keys_all.shape[0], dtype=jnp.int32) < length
        mixed, logsums = group_forward(queries, keys_all, values_all, valid_keys, group_width)
    bias_up = vector_rows[8:].reshape(-1)
    resid_one = (
        inputs.astype(jnp.float32)
        + jnp.dot(mixed, weight_out, preferred_element_type=jnp.float32)
        + vector_rows[2]
    )
    hidden, normed_one, inverse_one = norm_forward(resid_one, vector_rows[3], vector_rows[4])
    hidden_low = hidden.astype(jnp.bfloat16)
    preact = jnp.dot(hidden_low, weight_up, preferred_element_type=jnp.float32) + bias_up
    activ_full, gelu_slope = gelu_parts(preact)
    activated = activ_full.astype(jnp.bfloat16)
    resid_two = hidden + contract_cols(activated, weight_down) + vector_rows[5]
    outputs, normed_two, inverse_two = norm_forward(resid_two, vector_rows[6], vector_rows[7])
    grad_resid_two = norm_backward(upstream, vector_rows[6], normed_two, inverse_two)
    grad_two_low = grad_resid_two.astype(jnp.bfloat16)
    if by_heads:
        weight_qkv = all_rows(lax.optimization_barrier((rows_qkv, packed))[0])
    order = reordered(inputs)
    line.mark(grad_two_low)
    down_grads = chain(scatter_grads, grad_two_low, activated, order)
    grad_preact = jnp.dot(line.tie(grad_two_low), weight_down, preferred_element_type=jnp.float32)
    grad_preact = grad_preact * gelu_slope
    grad_preact_low = line.mark(grad_preact.astype(jnp.bfloat16))
    up_grads = chain(scatter_grads, hidden_low, grad_preact_low, order)
    down_grads.step()
    grad_hidden = grad_resid_two + contract_cols(line.tie(grad_preact_low), weight_up)
    grad_resid_one = norm_backward(grad_hidden, vector_rows[3], normed_one, inverse_one)
    grad_one_low = grad_resid_one.astype(jnp.bfloat16)
    grad_mixed = contract_cols(grad_one_low, weight_out).astype(jnp.bfloat16)
    line.mark(grad_mixed)
    def vector_terms(query_sum, value_sum):
        small_rows = jnp.stack(
            [
                query_sum,
                value_sum,
                jnp.sum(grad_resid_one, axis=0),
                jnp.sum(grad_hidden * normed_one, axis=0),
                jnp.sum(grad_hidden, axis=0),
                jnp.sum(grad_resid_two, axis=0),
                jnp.sum(upstream * normed_two, axis=0),
                jnp.sum(upstream, axis=0),
            ]
        )
        return jnp.concatenate(
            [small_rows, jnp.sum(grad_preact, axis=0).reshape(-1, width)], axis=0
        )

    if by_heads:
        grad_all = to_heads(grad_mixed, 1)
        out_grads = chain(scatter_grads, mixed, grad_one_low, order)
        up_grads.step()
        down_grads.step()
        out_grads.step()
        grad_heads = attend_back(packed, lengths, mixed_heads, logsums, line.tie(grad_all))
        line.mark(grad_heads)
        grad_proj = to_positions(grad_heads, 3)
        sums = jnp.sum(grad_heads.astype(jnp.float32), axis=0).reshape(3, wide)
        all_sums = jnp.zeros((3, groups, wide), jnp.float32)
        all_sums = lax.dynamic_update_index_in_dim(all_sums, sums, lax.axis_index(CTX), 1)
        all_sums = all_sums.reshape(3, width)
        query_sum, value_sum = all_sums[0], all_sums[2]
        grad_cols = jnp.concatenate(
            [contract_rows(tokens_left, grad_heads), contract_rows(tokens_right, grad_heads)]
        ).astype(jnp.bfloat16)
        heads_chain = chain(
            heads_grads, grad_cols, vector_terms(query_sum, value_sum), grad_proj, groups, wide
        )
        up_grads.step()
        heads_chain.step()
        down_grads.step()
        out_grads.step()
        heads_chain.step()
        up_grads.step()
        out_grads.step()
    else:
        up_grads.step()
        out_grads = chain(scatter_grads, mixed, grad_one_low, order)
        for made in (down_grads, up_grads) * 2 + (out_grads,) * 3:
            made.step()
        grad_query, key_terms, value_terms = group_backward(
            queries, keys_all, values_all, mixed, grad_mixed, logsums, valid_keys, group_width
        )
        grad_key, grad_value = (
            lax.psum_scatter(
                terms.astype(jnp.bfloat16), CTX, scatter_dimension=0, tiled=True
            ).astype(jnp.float32)
            for terms in (key_terms, value_terms)
        )
        grad_proj = jnp.concatenate([grad_query, grad_key, grad_value], axis=1).astype(jnp.bfloat16)
        query_sum, value_sum = jnp.sum(grad_query, axis=0), jnp.sum(grad_value, axis=0)
        qkv_grads = chain(scatter_grads, inputs, grad_proj, order)
        for _ in range(3):
            qkv_grads.step()
    grad_input = grad_resid_one + contract_cols(grad_proj, weight_qkv)
    if by_heads:
        grad_qkv, grad_vectors = heads_chain.step().value
    else:
        grad_qkv = qkv_grads.step().value
        vec_blocks = vector_terms(query_sum, value_sum)
        vec_blocks = vec_blocks.reshape(vector_count, lax.axis_size(EVERY), -1).transpose(1, 0, 2)
        grad_vectors = jnp.sum(lax.all_to_all(vec_blocks, EVERY, 0, 0, tiled=True), axis=0)
    grad_down = down_grads.step().value
    grad_up = up_grads.step().value
    grad_out = out_grads.step().value
    grad_matrices = jnp.concatenate([grad_qkv, grad_out, grad_up, grad_down], axis=1)
    new_matrices, new_first, new_second = adam_update(
        matrices, grad_matrices, first_moment, second_moment, decay_rate
    )
    new_vectors, new_vec_first, new_vec_second = adam_update(
        vectors, grad_vectors, vec_first, vec_second, 0.0
    )
    return (
        outputs[None],
        grad_input[None],
        grad_matrices,
        grad_vectors,
        new_matrices,
        new_vectors,
        new_first,
        new_second,
        new_vec_first,
        new_vec_second,
    )


def solution(mesh):
    ctx, shard = mesh.shape["ctx"], mesh.shape["shard"]
    mesh = Mesh(mesh.devices.reshape(ctx // 2, 2, shard // 2, 2), EVERY)
    placed = (
        P(("x", "c"), CTX, None),
        P(("x", "c"), CTX, None),
        P(("x", "c")),
        P(EVERY, None),
        P(None, EVERY),
        P(EVERY, None),
        P(EVERY, None),
        P(None, EVERY),
        P(None, EVERY),
    )
    return jax.shard_map(
        local,
        mesh=mesh,
        in_specs=placed,
        out_specs=(
            P(("x", "c"), CTX, None),
            P(("x", "c"), CTX, None),
            P(EVERY, None),
            P(None, EVERY),
            P(EVERY, None),
            P(None, EVERY),
            P(EVERY, None),
            P(EVERY, None),
            P(None, EVERY),
            P(None, EVERY),
        ),
        check_vma=False,
    )
```
